256 devices in a mesh: seq: 32 (over x, z), ch: 8 (over y, core).
Axes of the slice: x: 4, y: 4, z: 8, core: 2. Of those that a mesh axis runs over, the one named last changes fastest.
Arguments:
- features: bfloat16 [32768, 1024], P('seq', 'ch'), may hold values from -6 to 6
- w_qkv: bfloat16 [1024, 3072], P('ch'), may hold values from -0.1875 to 0.1875
- log_gate: float32 [8, 32768], P(None, ('seq', 'ch')), may hold values from -1 to 0
- norm_gain: float32 [1024], replicated, may hold values from 0.1 to 1.9
- w_pred: bfloat16 [4, 1024, 1024], replicated, may hold values from -0.1875 to 0.1875
- patch_mask: int32 [32768], P(('seq', 'ch')), may hold values 0 or 1
- neg_index: int32 [4, 256], P(None, ('seq', 'ch')), may hold values from 0 to 32767, as said below
Outputs:
- context: bfloat16 [32768, 1024], P(('seq', 'ch'))
- nce_loss: float32 [4, 32768], P(None, ('seq', 'ch'))
The draws below stay inside these ranges and needn't reach their ends.
Inputs may be any that keep to these rules, and one draw needn't show every extreme that they name: `neg_index`: negative n of every offset lies among the 128 patches of block n, blocks of 128 consecutive patches.
All inputs are finite; a program needn't handle non-finite values. No bound on the sum of `patch_mask` on one device may be relied on, other than what follows from the above.
Results may differ from the reference program's by a relative error of at most 0.0061.
Values may be sent and summed in bfloat16 or wider, within the bound.
No kernel may reach another device: no remote copies, remote signals or barrier semaphores. Data moves between devices by JAX's collectives and lax.ppermute only.
A program may use at most 320 MiB of HBM per device.

```python
import math
import jax
import jax.numpy as jnp
from jax import lax

CIN = 1024
HEADS = 8
HEAD_DIM = 128
K = 4
TOK_DEV = 128
NEG_DEV = 1
HD = 1024
ROW_W = 64
SLIDE_PATCHES = 32768
NNEG = 256


def draw_log_gate(key, part):
    portion_count = jax.random.split(key, 8)
    fast_count = jax.random.randint(portion_count[0], (), 1, HEADS)
    order = jax.random.permutation(portion_count[1], HEADS)
    fast = (order < fast_count).astype(jnp.float32)
    fast_rate = jnp.exp(jax.random.uniform(portion_count[2], (HEADS,), jnp.float32, math.log(1.0 / 50.0), math.log(1.0 / 30.0)))
    slow_rate = jnp.exp(jax.random.uniform(portion_count[3], (HEADS,), jnp.float32, math.log(0.02), math.log(0.25))) * (math.log(10.0) / SLIDE_PATCHES)
    arrival_rate = fast * fast_rate + (1.0 - fast) * slow_rate
    token_multiplier = jax.random.uniform(portion_count[4], (HEADS, SLIDE_PATCHES), jnp.float32, 0.5, 1.5)
    block_multiplier = jnp.exp(jax.random.uniform(portion_count[5], (HEADS, SLIDE_PATCHES // TOK_DEV, 1), jnp.float32, math.log(0.5), math.log(2.0)))
    block_multiplier = jnp.broadcast_to(block_multiplier, (HEADS, SLIDE_PATCHES // TOK_DEV, TOK_DEV)).reshape(HEADS, SLIDE_PATCHES)
    spike_position = jax.random.randint(portion_count[6], (3,), 0, SLIDE_PATCHES)
    spike_length = jnp.log(jax.random.uniform(portion_count[7], (3, 1), jnp.float32, 0.5, 0.8))
    match_count = jnp.arange(SLIDE_PATCHES)[None, :] == spike_position[:, None]
    spike_event = jnp.sum(jnp.where(match_count, spike_length, 0.0), axis=0)
    return -arrival_rate[:, None] * token_multiplier * block_multiplier + spike_event[None, :]


def draw_neg_index(key, part):
    offsets = jax.random.randint(key, (K, NNEG), 0, TOK_DEV)
    column = jnp.arange(NNEG)[None, :]
    row = jnp.arange(K)[:, None]
    chosen = column // NEG_DEV * TOK_DEV + offsets
    first = (row == 0) & (column == 0)
    last = (row == 0) & (column == NNEG - 1)
    chosen = jnp.where(first, 0, chosen)
    chosen = jnp.where(last, SLIDE_PATCHES - 1, chosen)
    return chosen.astype(jnp.int32)


def plant(drawn, key, least, top_value):
    index_at = [jax.random.randint(jax.random.fold_in(key, axis), (), 0, length) for axis, length in enumerate(drawn.shape)]
    longest = drawn.shape.index(max(drawn.shape))
    neighbour = index_at[:longest] + [(index_at[longest] + 1) % drawn.shape[longest]] + index_at[longest + 1:]
    return drawn.at[tuple(index_at)].set(least).at[tuple(neighbour)].set(top_value)


def block_levels(rng, dims, cuts, smallest, largest):
    def one(dim, blocks):
        draws = jax.random.uniform(jax.random.fold_in(jax.random.fold_in(rng, 6), dim), (blocks,), jnp.float32, smallest / len(cuts), largest / len(cuts))
        return jnp.repeat(jnp.exp(draws), dims[dim] // blocks).reshape((-1,) + (1,) * (len(dims) - dim - 1))

    level = one(*cuts[0])
    for cut in cuts[1:]:
        level = level * one(*cut)
    return level


def noise(rng, dims, width, most, pieces=(), held_as=jnp.bfloat16):
    result = width * jax.random.normal(rng, dims, jnp.float32)
    if pieces:
        result = result * block_levels(rng, dims, pieces, -0.22, 0.18)
    return jnp.clip(result, -most, most).astype(held_as)


def setup_inputs(seed: int = 0) -> dict:
    seeds = jax.random.split(jax.random.key(seed), 8)
    return {
        "features": noise(seeds[0], (SLIDE_PATCHES, CIN), 1.0, 6.0, ((0, 32), (1, 8))),
        "w_qkv": noise(seeds[1], (CIN, 3 * HD), CIN ** -0.5, 0.1875, ((0, 8),)),
        "log_gate": draw_log_gate(jax.random.fold_in(seeds[7], 71), 0),
        "norm_gain": jnp.clip(1.0 + 0.18 * jax.random.normal(seeds[3], (HD,), jnp.float32), 0.1, 1.9),
        "w_pred": noise(seeds[4], (K, HD, CIN), HD ** -0.5, 0.1875),
        "patch_mask": plant((jax.random.randint(seeds[5], (SLIDE_PATCHES,), 0, 8) < 7).astype(jnp.int32), jax.random.fold_in(seeds[5], 1), 0, 1),
        "neg_index": draw_neg_index(jax.random.fold_in(seeds[7], 71), 0),
    }


def reference(features, w_qkv, log_gate, norm_gain, w_pred, patch_mask, neg_index):
    inner = HEADS * HEAD_DIM
    highest = lax.Precision.HIGHEST
    score_scale = 4.0 * CIN ** (-0.5)
    projected = jnp.dot(features, w_qkv, preferred_element_type=jnp.float32).astype(jnp.bfloat16)
    mask_wire = patch_mask.astype(jnp.bfloat16)
    queries = projected[:, :inner].astype(jnp.float32)
    keys_all = projected[:, inner:2 * inner].astype(jnp.float32)
    values = (projected[:, 2 * inner:] * mask_wire[:, None]).astype(jnp.float32)
    blocks = SLIDE_PATCHES // TOK_DEV
    q_blocks = queries.reshape(blocks, TOK_DEV, HEADS, HEAD_DIM)
    k_blocks = keys_all.reshape(blocks, TOK_DEV, HEADS, HEAD_DIM)
    v_blocks = values.reshape(blocks, TOK_DEV, HEADS, HEAD_DIM)
    g_blocks = jnp.transpose(log_gate.reshape(HEADS, blocks, TOK_DEV), (1, 0, 2))
    lower = jnp.arange(TOK_DEV)[:, None] >= jnp.arange(TOK_DEV)[None, :]

    def step(state, inputs):
        q_part, k_part, v_part, g_part = inputs
        cumul = jnp.cumsum(g_part, axis=1)
        scores = jnp.einsum('thd,shd->hts', q_part, k_part, precision=highest)
        diff = cumul[:, :, None] - cumul[:, None, :]
        decay = jnp.where(lower[None], jnp.exp(jnp.where(lower[None], diff, 0.0)), 0.0)
        intra = jnp.einsum('hts,shd->thd', scores * decay, v_part, precision=highest)
        inter = jnp.einsum('thd,hde->the', q_part, state, precision=highest) * jnp.exp(cumul).T[:, :, None]
        tail = jnp.exp(cumul[:, -1:] - cumul)
        summary = jnp.einsum('shd,she->hde', k_part * tail.T[:, :, None], v_part, precision=highest)
        new_state = jnp.exp(cumul[:, -1])[:, None, None] * state + summary
        return (new_state, (intra + inter) * HEAD_DIM ** (-0.5))
    start_state = jnp.zeros((HEADS, HEAD_DIM, HEAD_DIM), jnp.float32)
    _, mixed = lax.scan(step, start_state, (q_blocks, k_blocks, v_blocks, g_blocks))
    mixed = mixed.reshape(SLIDE_PATCHES, HEADS, HEAD_DIM)
    squares = lax.optimization_barrier(jnp.mean(mixed * mixed, axis=-1, keepdims=True))
    normed = (mixed / jnp.sqrt(squares + 1e-06)).reshape(SLIDE_PATCHES, inner)
    context = (normed * norm_gain).astype(jnp.bfloat16)
    maskf = patch_mask.astype(jnp.float32)
    padded = jnp.concatenate([features, jnp.zeros((K * ROW_W, CIN), jnp.bfloat16)], axis=0)
    mask_pad = jnp.concatenate([maskf, jnp.zeros((K * ROW_W,), jnp.float32)], axis=0)
    losses = []
    for offset in range(K):
        predicted = jnp.dot(context, w_pred[offset], preferred_element_type=jnp.float32).astype(jnp.bfloat16)
        shift_rows = (offset + 1) * ROW_W
        target = lax.dynamic_slice_in_dim(padded, shift_rows, SLIDE_PATCHES, 0)
        target_mask = lax.dynamic_slice_in_dim(mask_pad, shift_rows, SLIDE_PATCHES, 0)
        positive = jnp.einsum('tc,tc->t', predicted.astype(jnp.float32), target.astype(jnp.float32)) * score_scale
        bank = jnp.take(features, neg_index[offset], axis=0)
        logits = jnp.dot(predicted, bank.T, preferred_element_type=jnp.float32) * score_scale
        negsum = lax.optimization_barrier(jnp.sum(jnp.exp(logits), axis=1))
        valid = maskf * target_mask
        losses.append(valid * (jnp.log(jnp.exp(positive) + negsum) - positive))
    return (context, jnp.stack(losses, axis=0))
```

```python
import jax
import jax.numpy as jnp
from jax import lax
from jax.sharding import PartitionSpec as P

CIN = 1024
HEADS = 8
HEAD_DIM = 128
K = 4
ROW = 64
NORM_EPS = 1e-06
F32 = jnp.float32
BF16 = jnp.bfloat16
BOTH = ("seq", "ch")


def exchange(x, axis, groups=None):
    return lax.all_to_all(x, axis, split_axis=0, concat_axis=0, axis_index_groups=groups)


def collect(x, axis, size, groups=None):
    return exchange(jnp.broadcast_to(x[None], (size,) + x.shape), axis, groups)


def shards(features, w_qkv, log_gate, norm_gain, w_pred, patch_mask, neg_index):
    nseq, nch = lax.axis_size("seq"), lax.axis_size("ch")
    block = features.shape[0]
    length = block // nch
    xs, zs = 4, nseq // 4
    along_z = [[x * zs + z for z in range(zs)] for x in range(xs)]
    along_x = [[x * zs + z for x in range(xs)] for z in range(zs)]
    seq_at, ch_at = lax.axis_index("seq"), lax.axis_index("ch")
    x_at, z_at = seq_at // zs, seq_at % zs
    score_scale = 4.0 * CIN ** (-0.5)

    place = neg_index[:, 0] - seq_at * block
    small = jnp.concatenate(
        [
            log_gate[:, None, :],
            jnp.broadcast_to(patch_mask.astype(F32)[None, None], (nch, 1, length)),
            jnp.broadcast_to(jnp.pad(place.astype(F32), (0, length - K))[None, None], (nch, 1, length)),
        ],
        axis=1,
    )
    small = exchange(small, "ch")
    gate = small[:, 0].reshape(block)
    mask = small[:, 1].reshape(block)
    rows = small[:, 2, :K].astype(jnp.int32)

    encoded = collect(features, "ch", nch)
    w_mine = exchange(
        w_qkv.reshape(w_qkv.shape[0], 3, nch, HEAD_DIM).transpose(2, 0, 1, 3).reshape(nch, w_qkv.shape[0], 3 * HEAD_DIM),
        "ch",
    )

    picked = jnp.take(features, rows.T.reshape(-1), axis=0).reshape(K, nch, -1)
    bank = collect(picked, "seq", nseq)
    bank = bank.transpose(1, 0, 2, 3).reshape(K, nseq * nch, -1)
    bank = collect(bank, "ch", nch)

    projected = jnp.einsum("ctk,ckn->tn", encoded, w_mine, preferred_element_type=F32).astype(BF16)
    queries = projected[:, :HEAD_DIM]
    keys = projected[:, HEAD_DIM : 2 * HEAD_DIM]
    values = projected[:, 2 * HEAD_DIM :] * mask.astype(BF16)[:, None]
    cumul = jnp.cumsum(gate)
    total = cumul[-1]
    tail = jnp.exp(total - cumul)
    summary = jnp.einsum(
        "sd,se->de", (keys.astype(F32) * tail[:, None]).astype(BF16), values, preferred_element_type=F32
    )
    totals = lax.all_to_all(
        jnp.broadcast_to(total, (nseq, 1, 128)), "seq", split_axis=0, concat_axis=0
    )[:, 0, 0].reshape(xs, zs)
    in_z = collect(summary.astype(BF16), "seq", zs, along_z)
    mine = lax.dynamic_index_in_dim(totals, x_at, 0, False)
    zi = jnp.arange(zs)
    below = zi[None, :] < zi[:, None]
    acc = jnp.cumsum(mine)
    before = jnp.concatenate([jnp.zeros((1,), F32), acc[:-1]])
    w_row = jnp.exp(acc[-1] - acc)
    w_here = jnp.where(zi < z_at, jnp.exp(jnp.where(zi < z_at, before[z_at] - acc, 0.0)), 0.0)
    both = jnp.einsum("wz,zde->wde", jnp.stack([w_row, w_here]), in_z.astype(F32), precision=lax.Precision.HIGHEST)
    in_x = collect(both[0].astype(BF16), "seq", xs, along_x)
    xi = jnp.arange(xs)
    row_acc = jnp.cumsum(jnp.sum(totals, axis=1))
    row_before = jnp.concatenate([jnp.zeros((1,), F32), row_acc[:-1]])
    w_x = jnp.where(
        xi < x_at, jnp.exp(jnp.where(xi < x_at, row_before[x_at] - row_acc, 0.0) + before[z_at]), 0.0
    )
    incoming = both[1] + jnp.einsum("x,xde->de", w_x, in_x.astype(F32), precision=lax.Precision.HIGHEST)

    lower = jnp.arange(block)[:, None] >= jnp.arange(block)[None, :]
    decay = jnp.where(lower, jnp.exp(jnp.where(lower, cumul[:, None] - cumul[None, :], 0.0)), 0.0)
    scores = jnp.einsum("td,sd->ts", queries, keys, preferred_element_type=F32)
    intra = jnp.einsum("ts,se->te", (scores * decay).astype(BF16), values, preferred_element_type=F32)
    inter = jnp.einsum("td,de->te", queries, incoming.astype(BF16), preferred_element_type=F32)
    mixed = (intra + inter * jnp.exp(cumul)[:, None]) * HEAD_DIM ** (-0.5)
    squares = jnp.mean(mixed * mixed, axis=-1, keepdims=True)
    gain = lax.dynamic_slice_in_dim(norm_gain, ch_at * HEAD_DIM, HEAD_DIM, 0)
    context = (mixed / jnp.sqrt(squares + NORM_EPS) * gain).astype(BF16)
    context = exchange(context.reshape(nch, length, HEAD_DIM), "ch")
    context = context.transpose(1, 0, 2).reshape(length, HEADS * HEAD_DIM)

    ahead = encoded[:, : K * ROW]
    ahead = jnp.concatenate(
        [ahead, jnp.broadcast_to(mask[: K * ROW].astype(BF16)[None, None], (nch, 1, K * ROW))[:, :, :128],
         jnp.broadcast_to(mask[: K * ROW].astype(BF16)[None, None], (nch, 1, K * ROW))[:, :, 128:]], axis=1)
    last = nch - 2
    pairs = [((s + 1) * nch + c, s * nch + c) for s in range(nseq - 1) for c in range(last, nch)]
    ahead = lax.ppermute(ahead, BOTH, pairs)
    mask_next = jnp.concatenate([ahead[0, K * ROW], ahead[0, K * ROW + 1]]).astype(F32)
    window = jnp.concatenate([encoded, ahead[:, : K * ROW]], axis=1)
    window = lax.dynamic_slice_in_dim(window, ch_at * length, length + K * ROW, 1)
    flags = lax.dynamic_slice_in_dim(
        jnp.concatenate([mask, mask_next]), ch_at * length, length + K * ROW, 0
    )

    losses = []
    for j in range(K):
        predicted = jnp.dot(context, w_pred[j], preferred_element_type=F32).astype(BF16)
        parts = predicted.reshape(length, nch, 128)
        logits = jnp.einsum("tck,cnk->tn", parts, bank[:, j], preferred_element_type=F32) * score_scale
        negsum = jnp.sum(jnp.exp(logits), axis=1)
        target = window[:, (j + 1) * ROW : (j + 1) * ROW + length]
        positive = (
            jnp.einsum("tck,ctk->t", parts.astype(F32), target.astype(F32)) * score_scale
        )
        valid = flags[:length] * flags[(j + 1) * ROW : (j + 1) * ROW + length]
        losses.append(valid * (jnp.log(jnp.exp(positive) + negsum) - positive))
    return (context, jnp.stack(losses, axis=0))


def solution(mesh):
    placed = (
        P("seq", "ch"),
        P("ch", None),
        P(None, BOTH),
        P(),
        P(),
        P(BOTH),
        P(None, BOTH),
    )
    return jax.shard_map(
        shards,
        mesh=mesh,
        in_specs=placed,
        out_specs=(P(BOTH, None), P(None, BOTH)),
        check_vma=False,
    )
```

```python
import jax
import jax.numpy as jnp
from jax import lax
from jax.experimental import pallas as pl
from jax.experimental.pallas import tpu as pltpu
from jax.sharding import PartitionSpec as P


CIN = 1024
HEADS = 8
D = 128
K = 4
ROW = 64
NORM_EPS = 1e-06
XS, ZS, YS = 4, 8, 4
NSEQ, NCH = XS * ZS, 2 * YS
LEN = 128
BLOCK = NCH * LEN
F32 = jnp.float32
BF16 = jnp.bfloat16
BOTH = ("seq", "ch")
ALONG_Z = [[x * ZS + z for z in range(ZS)] for x in range(XS)]
ALONG_X = [[x * ZS + z for x in range(XS)] for z in range(ZS)]
SCORE_SCALE = 4.0 * CIN ** (-0.5)

VMEM = pl.BlockSpec(memory_space=pltpu.VMEM)


def call(body, out, ins, flops=0, scratch=(), after=()):
    n = len(ins)

    def kernel(*refs):
        body(*refs[:n], *refs[n + len(after) :])

    moved = sum(a.size * a.dtype.itemsize for a in ins) + sum(o.size * o.dtype.itemsize for o in out)
    return pl.pallas_call(
        kernel,
        out_shape=out,
        in_specs=[VMEM] * n + [pl.BlockSpec(memory_space=pl.ANY)] * len(after),
        out_specs=[VMEM] * len(out),
        scratch_shapes=list(scratch),
        cost_estimate=pl.CostEstimate(flops=flops, bytes_accessed=moved, transcendentals=0),
    )(*ins, *after)


def place():
    s, c = lax.axis_index("seq"), lax.axis_index("ch")
    return s >> 3, s & (ZS - 1), c >> 1, c & 1


def shape(dims, dtype):
    return jax.ShapeDtypeStruct(dims, dtype)


def exchange(x, axis, groups=None):
    return lax.all_to_all(x, axis, split_axis=0, concat_axis=0, axis_index_groups=groups)


def hop(x, dy, swap=False):
    pairs = []
    for c in range(NCH):
        y, k = c // 2, c % 2
        pairs.append((c, ((y + dy) % YS) * 2 + ((1 - k) if swap else k)))
    return lax.ppermute(x, "ch", pairs)


def spread(x):
    half = x.shape[0] // 2
    up, dn = hop(x, 1), hop(x, -1)
    other = hop(x, 0, True)
    far_a, far_b = hop(up[:half], 1), hop(dn[half:], -1)
    return [x, up, dn, far_a, far_b], [other] + [hop(a, 0, True) for a in (up, dn, far_a, far_b)]


def split3(x):
    hi = x.astype(BF16).astype(F32)
    mid = (x - hi).astype(BF16).astype(F32)
    return hi, mid, x - hi - mid


PART = LEN


def pack_kernel(w, gate, mask, neg, out):
    hi, mid, lo = split3(gate[...])
    m = mask[...].astype(F32)
    spot = neg[...] - lax.axis_index("seq") * BLOCK
    p_hi, p_lo = (spot >> 5).astype(F32), (spot & 31).astype(F32)
    row = lax.broadcasted_iota(jnp.int32, (16, LEN), 0)
    mine = w[...]
    for h in range(HEADS):
        for part in range(3):
            out[h, 0:PART, part * D : (part + 1) * D] = mine[:, (part * HEADS + h) * D : (part * HEADS + h + 1) * D]
        a = jnp.where(row == 0, hi[h : h + 1], 0.0) + jnp.where(row == 1, m, 0.0)
        b = jnp.where(row == 0, mid[h : h + 1], 0.0)
        c = jnp.where(row == 0, lo[h : h + 1], 0.0)
        for j in range(K):
            a = a + jnp.where(row == 2 + j, p_hi[:, j : j + 1], 0.0)
            b = b + jnp.where(row == 2 + j, p_lo[:, j : j + 1], 0.0)
        out[h, PART : PART + 16, 0:D] = a.astype(BF16)
        out[h, PART : PART + 16, D : 2 * D] = b.astype(BF16)
        out[h, PART : PART + 16, 2 * D : 3 * D] = c.astype(BF16)


def homes(y):
    return [y, (y + 3) % YS, (y + 1) % YS, (y + 2) % YS]


def column(a, r):
    return jnp.concatenate([a[:, 2 * r : 2 * r + 1], a[:, 2 * r + 1 : 2 * r + 2]], axis=0)


def paired(w, first, last):
    _, _, y_at, core = place()
    return [
        jnp.concatenate([w[2 * y + core, 0:LEN, first:last], w[2 * y + 1 - core, 0:LEN, first:last]], axis=0)
        for y in homes(y_at)
    ]


def encoded_dot(mine, theirs, pairs, lo, size):
    acc = None
    for i in range(4):
        k, at = (i, lo) if i < 3 else (3, lo) if lo < BLOCK // 2 else (4, lo - BLOCK // 2)
        both = jnp.concatenate([mine[k][at : at + size], theirs[k][at : at + size]], axis=1)
        term = jnp.dot(both, pairs[i], preferred_element_type=F32)
        acc = term if acc is None else acc + term
    return acc


def project_kernel(part, *refs):
    mine, theirs = refs[0:5], refs[5:10]
    k_out, v_out, packet, cum_out, mask_out = refs[10:15]
    gates, places = refs[15:17]
    for c in range(NCH):
        info = part[c, PART : PART + 16, :].astype(F32)
        for p in range(3):
            gates[p, c : c + 1, :] = info[0:1, p * D : (p + 1) * D]
        mask_out[c : c + 1, :] = info[1:2, 0:D]
        for j in range(K):
            places[j * NCH + c : j * NCH + c + 1, :] = info[2 + j : 3 + j, 0:D] * 32.0 + info[2 + j : 3 + j, D : 2 * D]
    tri = (
        lax.broadcasted_iota(jnp.int32, (LEN, LEN), 0) <= lax.broadcasted_iota(jnp.int32, (LEN, LEN), 1)
    ).astype(BF16)
    cum = sum(jnp.dot(gates[p].astype(BF16), tri, preferred_element_type=F32) for p in range(3))
    rows, offset = [], jnp.zeros((1, 1), F32)
    for c in range(NCH):
        rows.append(cum[c : c + 1] + offset)
        offset = rows[-1][:, LEN - 1 : LEN]
    cum = jnp.concatenate(rows, axis=0)
    total = offset
    cum_out[...] = cum
    tail_t = jnp.exp(total - cum).T
    mask_t = mask_out[...].T
    pairs = paired(part, D, 3 * D)
    state = jnp.zeros((D, D), F32)
    size = 256
    for r in range(BLOCK // size):
        lo = r * size
        acc = encoded_dot(mine, theirs, pairs, lo, size)
        keys = acc[:, 0:D].astype(BF16)
        k_out[lo : lo + size] = keys
        values = (acc[:, D:].astype(BF16).astype(F32) * column(mask_t, r)).astype(BF16)
        v_out[lo : lo + size] = values
        scaled = (keys.astype(F32) * column(tail_t, r)).astype(BF16)
        state += lax.dot_general(scaled, values, (((0,), (0,)), ((), ())), preferred_element_type=F32)
    hot = (places[:, 0:1].astype(jnp.int32) == lax.broadcasted_iota(jnp.int32, (K * NCH, BLOCK), 1)).astype(F32)
    picked = jnp.dot(hot.astype(BF16), mine[0][...], preferred_element_type=F32).astype(BF16)
    row = lax.broadcasted_iota(jnp.int32, (16, D), 0)
    hi, mid, low = split3(total)
    info = (jnp.where(row == 0, hi, 0.0) + jnp.where(row == 1, mid, 0.0) + jnp.where(row == 2, low, 0.0)).astype(BF16)
    state = state.astype(BF16)
    for z in range(ZS):
        packet[z, 0:D, :] = state
        packet[z, D : D + 16, :] = info
        packet[z, D + 16 : D + 16 + K * NCH, :] = picked


FAR = K * ROW


def intra_kernel(part, *refs):
    mine, theirs = refs[0:5], refs[5:10]
    k, v, cum, masks = refs[10:14]
    q, out, window, halo = refs[14:18]
    pairs = paired(part, 0, D)
    size = 256
    cum_rows = cum[...]
    cum_t = cum_rows.T
    lower = lax.broadcasted_iota(jnp.int32, (size, size), 0) >= lax.broadcasted_iota(jnp.int32, (size, size), 1)
    for r in range(BLOCK // size):
        here = column(cum_t, r)
        queries = encoded_dot(mine, theirs, pairs, r * size, size).astype(BF16)
        q[r * size : (r + 1) * size] = queries
        acc = jnp.zeros((size, D), F32)
        for s in range(r + 1):
            diff = here - jnp.concatenate([cum_rows[2 * s : 2 * s + 1], cum_rows[2 * s + 1 : 2 * s + 2]], axis=1)
            if s == r:
                diff = jnp.where(lower, diff, -jnp.inf)
            scores = lax.dot_general(
                queries, k[s * size : (s + 1) * size], (((1,), (1,)), ((), ())), preferred_element_type=F32
            )
            acc += jnp.dot((scores * jnp.exp(diff)).astype(BF16), v[s * size : (s + 1) * size], preferred_element_type=F32)
        out[r * size : (r + 1) * size] = acc
    _, _, y_at, core = place()
    ys = homes(y_at)
    for b in range(3):
        at_row = 2 * y_at + core + b
        inside = jnp.minimum(at_row, NCH - 1)
        low = pl.ds(pl.multiple_of(jnp.minimum(inside, 3) * LEN, LEN), LEN)
        high = pl.ds(pl.multiple_of(jnp.maximum(inside - 4, 0) * LEN, LEN), LEN)
        rows = pl.ds(pl.multiple_of(inside * LEN, LEN), LEN)
        for i, y in enumerate(ys):
            for who, group in ((core, mine), (1 - core, theirs)):
                lanes = pl.ds(pl.multiple_of((2 * y + who) * D, D), D)
                if i < 3:
                    window[b * LEN : (b + 1) * LEN, lanes] = group[i][rows, :]
                else:
                    window[b * LEN : (b + 1) * LEN, lanes] = jnp.where(inside < 4, group[3][low, :], group[4][high, :])
    for i, y in enumerate(ys):
        for who, group in ((core, mine), (1 - core, theirs)):
            halo[pl.ds(pl.multiple_of((2 * y + who) * FAR, FAR), FAR), :] = group[i][0:FAR, :]
    row = lax.broadcasted_iota(jnp.int32, (16, D), 0)
    halo[NCH * FAR : NCH * FAR + 16, :] = (
        jnp.where(row == 0, masks[0:1], 0.0) + jnp.where(row == 1, masks[1:2], 0.0)
    ).astype(BF16)


def log_of(block):
    info = block.astype(F32)
    return info[0:1] + info[1:2] + info[2:3]


def row_kernel(z_in, packet, here_out, before_out):
    z_at = place()[1]
    row_state, here = jnp.zeros((D, D), F32), jnp.zeros((D, D), F32)
    row_log, before = jnp.zeros((1, D), F32), jnp.zeros((1, D), F32)
    for z in range(ZS):
        log = log_of(z_in[z, D : D + 16, :])
        factor, state = jnp.exp(log), z_in[z, 0:D, :].astype(F32)
        row_state = row_state * factor + state
        row_log = row_log + log
        here = jnp.where(z < z_at, here * factor + state, here)
        before = jnp.where(z < z_at, before + log, before)
    here_out[...] = here
    before_out[...] = jnp.broadcast_to(before, (8, D))
    row = lax.broadcasted_iota(jnp.int32, (16, D), 0)
    hi, mid, low = split3(row_log)
    info = (jnp.where(row == 0, hi, 0.0) + jnp.where(row == 1, mid, 0.0) + jnp.where(row == 2, low, 0.0)).astype(BF16)
    row_state = row_state.astype(BF16)
    n = K * NCH
    for x in range(XS):
        packet[x, 0:D, :] = row_state
        packet[x, D : D + 16, :] = info
        for z in range(ZS):
            packet[x, D + 16 + z * n : D + 16 + (z + 1) * n, :] = z_in[z, D + 16 : D + 16 + n, :]


def finish_kernel(x_in, here, before, q, intra, cum, gain, out):
    x_at = place()[0]
    state = jnp.zeros((D, D), F32)
    for x in range(XS):
        log = log_of(x_in[x, D : D + 16, :])
        state = jnp.where(x < x_at, state * jnp.exp(log) + x_in[x, 0:D, :].astype(F32), state)
    incoming = (state * jnp.exp(before[0:1]) + here[...]).astype(BF16)
    grow_t = jnp.exp(cum[...]).T
    scale = gain[:, pl.ds(pl.multiple_of(lax.axis_index("ch") * D, D), D)]
    size = 256
    for r in range(BLOCK // size):
        grow = jnp.concatenate([grow_t[:, 2 * r : 2 * r + 1], grow_t[:, 2 * r + 1 : 2 * r + 2]], axis=0)
        inter = jnp.dot(q[r * size : (r + 1) * size], incoming, preferred_element_type=F32)
        mixed = (intra[r * size : (r + 1) * size] + inter * grow) * D ** (-0.5)
        squares = jnp.mean(mixed * mixed, axis=-1, keepdims=True)
        context = (mixed / jnp.sqrt(squares + NORM_EPS) * scale).astype(BF16)
        out[2 * r] = context[0:LEN]
        out[2 * r + 1] = context[LEN:]


def predict_kernel(ctx, w, context, predicted):
    j = pl.program_id(0)
    whole = jnp.concatenate([ctx[h] for h in range(HEADS)], axis=1)

    @pl.when(j == 0)
    def _():
        context[...] = whole

    predicted[0] = jnp.dot(whole, w[0], preferred_element_type=F32).astype(BF16)


def predict(ctx, w_pred):
    return pl.pallas_call(
        predict_kernel,
        grid=(K,),
        out_shape=[shape((LEN, CIN), BF16), shape((K, LEN, CIN), BF16)],
        in_specs=[pl.BlockSpec((HEADS, LEN, D), lambda j: (0, 0, 0)), pl.BlockSpec((1, CIN, CIN), lambda j: (j, 0, 0))],
        out_specs=[pl.BlockSpec((LEN, CIN), lambda j: (0, 0)), pl.BlockSpec((1, LEN, CIN), lambda j: (j, 0, 0))],
        name="predict",
        cost_estimate=pl.CostEstimate(flops=K * 2 * LEN * CIN * CIN, bytes_accessed=K * 2 * CIN * CIN, transcendentals=0),
    )(ctx, w_pred)


def loss_kernel(predicted, window, halo, masks, *refs):
    mine, theirs = refs[0:5], refs[5:10]
    loss, bank, ahead = refs[10:13]
    _, _, y_at, core = place()
    half = BLOCK // 2
    for i, y in enumerate(homes(y_at)):
        for who, group in ((core, mine), (1 - core, theirs)):
            lanes = pl.ds(pl.multiple_of((2 * y + who) * D, D), D)
            if i < 3:
                bank[:, lanes] = group[i][...]
            else:
                bank[0:half, lanes] = group[3][...]
                bank[half:, lanes] = group[4][...]
    me = 2 * y_at + core
    next_rows = halo[NCH * FAR : NCH * FAR + 16, :].astype(F32)
    ahead[0:LEN, :] = window[0:LEN, :]
    flags = [masks[pl.ds(me, 1), :]]
    for b in (1, 2):
        beyond = jnp.maximum(me + b - NCH, 0)

        @pl.when(me + b < NCH)
        def _():
            ahead[b * LEN : (b + 1) * LEN, :] = window[b * LEN : (b + 1) * LEN, :]

        @pl.when(me + b >= NCH)
        def _():
            for c in range(NCH):
                rows = pl.ds(pl.multiple_of(c * FAR + beyond * LEN, LEN), LEN)
                ahead[b * LEN : (b + 1) * LEN, c * D : (c + 1) * D] = halo[rows, :]

        outer = jnp.where(beyond == 0, next_rows[0:1], next_rows[1:2])
        flags.append(jnp.where(me + b < NCH, masks[pl.ds(jnp.minimum(me + b, NCH - 1), 1), :], outer))
    m0, m1, m2 = flags
    valid = [
        m0 * jnp.concatenate([m0[:, ROW:], m1[:, :ROW]], axis=1),
        m0 * m1,
        m0 * jnp.concatenate([m1[:, ROW:], m2[:, :ROW]], axis=1),
        m0 * m2,
    ]
    n = NSEQ * NCH
    for j in range(K):
        part = predicted[j]
        logits = (
            lax.dot_general(bank[j * n : (j + 1) * n, :], part, (((1,), (1,)), ((), ())), preferred_element_type=F32)
            * SCORE_SCALE
        )
        negsum = jnp.sum(jnp.exp(logits), axis=0, keepdims=True)
        acc = jnp.zeros((LEN, D), F32)
        for c in range(NCH):
            target = ahead[(j + 1) * ROW : (j + 1) * ROW + LEN, c * D : (c + 1) * D]
            acc += part[:, c * D : (c + 1) * D].astype(F32) * target.astype(F32)
        positive = jnp.sum(acc.T, axis=0, keepdims=True) * SCORE_SCALE
        loss[j : j + 1, :] = valid[j] * (jnp.log(jnp.exp(positive) + negsum) - positive)


def step(features, w_qkv, log_gate, norm_gain, w_pred, patch_mask, neg_index):
    mine, theirs = spread(features)
    (packed,) = call(
        pack_kernel, [shape((HEADS, PART + 16, 3 * D), BF16)],
        [w_qkv, log_gate, patch_mask.reshape(1, -1), neg_index.T],
    )
    w_part = exchange(packed, "ch")
    pieces = [w_part, *mine, *theirs]
    whole = shape((BLOCK, D), BF16)
    n = K * NCH
    keys, values, packet, cumul, masks = call(
        project_kernel,
        [whole, whole, shape((ZS, D + 16 + n, D), BF16), shape((NCH, LEN), F32), shape((NCH, LEN), F32)],
        pieces,
        flops=2 * BLOCK * CIN * 2 * D,
        scratch=[pltpu.VMEM((3, NCH, LEN), F32), pltpu.VMEM((n, D), F32)],
    )
    z_in = exchange(packet, "seq", ALONG_Z)
    queries, intra, window, halo = call(
        intra_kernel,
        [whole, shape((BLOCK, D), F32), shape((LEN + FAR, CIN), BF16), shape((NCH * FAR + 16, D), BF16)],
        [*pieces, keys, values, cumul, masks],
        flops=2 * BLOCK * (BLOCK + CIN) * D,
    )
    x_packet, here, before = call(
        row_kernel, [shape((XS, D + 16 + ZS * n, D), BF16), shape((D, D), F32), shape((8, D), F32)], [z_in],
        after=[intra],
    )
    x_packet, halo = lax.optimization_barrier((x_packet, halo))
    x_in = exchange(x_packet, "seq", ALONG_X)
    pairs = [((s + 1) * NCH + c, s * NCH + c) for s in range(NSEQ - 1) for c in (NCH - 2, NCH - 1)]
    halo = lax.ppermute(halo, BOTH, pairs)
    (context,) = call(
        finish_kernel, [shape((NCH, LEN, D), BF16)],
        [x_in, here, before, queries, intra, cumul, norm_gain.reshape(1, -1)], flops=2 * BLOCK * D * D,
    )
    bank = x_in[:, D + 16 :].reshape(XS * ZS, K, NCH, D).transpose(1, 0, 2, 3).reshape(K * NSEQ * NCH, D)
    context = exchange(context, "ch")
    bank_mine, bank_theirs = spread(bank)
    context, predicted = predict(context, w_pred)
    (loss,) = call(
        loss_kernel, [shape((K, LEN), F32)], [predicted, window, halo, masks, *bank_mine, *bank_theirs],
        flops=K * 2 * LEN * CIN * 256,
        scratch=[pltpu.VMEM((K * NSEQ * NCH, CIN), BF16), pltpu.VMEM((LEN + FAR, CIN), BF16)],
    )
    return context, loss


def solution(mesh):
    placed = (
        P("seq", "ch"),
        P("ch", None),
        P(None, BOTH),
        P(),
        P(),
        P(BOTH),
        P(None, BOTH),
    )
    return jax.shard_map(
        lambda *a: tuple(step(*a)),
        mesh=mesh,
        in_specs=placed,
        out_specs=(P(BOTH, None), P(None, BOTH)),
        check_vma=False,
    )
```

```python
import jax
import jax.numpy as jnp
from jax import lax
from jax.experimental import pallas as pl
from jax.experimental.pallas import tpu as pltpu
from jax.sharding import PartitionSpec as P


CIN = 1024
HEADS = 8
D = 128
K = 4
ROW = 64
NORM_EPS = 1e-06
XS, ZS, YS = 4, 8, 4
NSEQ, NCH = XS * ZS, 2 * YS
LEN = 128
BLOCK = NCH * LEN
F32 = jnp.float32
BF16 = jnp.bfloat16
BOTH = ("seq", "ch")
ALONG_Z = [[x * ZS + z for z in range(ZS)] for x in range(XS)]
ALONG_X = [[x * ZS + z for x in range(XS)] for z in range(ZS)]
GRANT = 20 * 1024 * 1024
SCORE_SCALE = 4.0 * CIN ** (-0.5)

VMEM = pl.BlockSpec(memory_space=pltpu.VMEM)
HBM = pl.BlockSpec(memory_space=pltpu.HBM)


def call(body, out, ins, flops=0, scratch=(), after=(), held=(), grant=True):
    n, m = len(ins), len(ins) + len(after) + len(out) + len(scratch)

    def kernel(*refs):
        given, rest = list(refs[:n]), refs[n + len(after) : m]
        if not held:
            return body(*given, *rest)
        copies = []
        for k, i in enumerate(held):
            copies.append(pltpu.make_async_copy(given[i], refs[m + k], refs[m + len(held) + k]))
            given[i] = refs[m + k]
        for copy in copies:
            copy.start()

        def wait():
            for copy in copies:
                copy.wait()

        body(wait, *given, *rest)

    moved = sum(a.size * a.dtype.itemsize for a in ins) + sum(o.size * o.dtype.itemsize for o in out)
    return pl.pallas_call(
        kernel,
        out_shape=out,
        in_specs=[HBM if i in held else VMEM for i in range(n)] + [pl.BlockSpec(memory_space=pl.ANY)] * len(after),
        out_specs=[VMEM] * len(out),
        scratch_shapes=[
            *scratch,
            *[pltpu.VMEM(ins[i].shape, ins[i].dtype) for i in held],
            *[pltpu.SemaphoreType.DMA for _ in held],
        ],
        cost_estimate=pl.CostEstimate(flops=flops, bytes_accessed=moved, transcendentals=0),
        compiler_params=pltpu.CompilerParams(vmem_limit_bytes=GRANT) if grant else None,
    )(*ins, *after)


def place():
    s, c = lax.axis_index("seq"), lax.axis_index("ch")
    return s >> 3, s & (ZS - 1), c >> 1, c & 1


def shape(dims, dtype):
    return jax.ShapeDtypeStruct(dims, dtype)


def exchange(x, axis, groups=None):
    return lax.all_to_all(x, axis, split_axis=0, concat_axis=0, axis_index_groups=groups)


def hop(x, dy, swap=False):
    pairs = []
    for c in range(NCH):
        y, k = c // 2, c % 2
        pairs.append((c, ((y + dy) % YS) * 2 + ((1 - k) if swap else k)))
    return lax.ppermute(x, "ch", pairs)


def spread(x):
    half = x.shape[0] // 2
    up, dn = hop(x, 1), hop(x, -1)
    other = hop(x, 0, True)
    far_a, far_b = hop(up[:half], 1), hop(dn[half:], -1)
    return [x, up, dn, far_a, far_b], [other] + [hop(a, 0, True) for a in (up, dn, far_a, far_b)]


def split3(x):
    hi = x.astype(BF16).astype(F32)
    mid = (x - hi).astype(BF16).astype(F32)
    return hi, mid, x - hi - mid


PART = LEN


def pack_kernel(w, gate, mask, neg, out):
    hi, mid, lo = split3(gate[...])
    m = mask[...].astype(F32)
    spot = neg[...] - lax.axis_index("seq") * BLOCK
    p_hi, p_lo = (spot >> 5).astype(F32), (spot & 31).astype(F32)
    row = lax.broadcasted_iota(jnp.int32, (16, LEN), 0)
    mine = w[...]
    for h in range(HEADS):
        for part in range(3):
            out[h, 0:PART, part * D : (part + 1) * D] = mine[:, (part * HEADS + h) * D : (part * HEADS + h + 1) * D]
        a = jnp.where(row == 0, hi[h : h + 1], 0.0) + jnp.where(row == 1, m, 0.0)
        b = jnp.where(row == 0, mid[h : h + 1], 0.0)
        c = jnp.where(row == 0, lo[h : h + 1], 0.0)
        for j in range(K):
            a = a + jnp.where(row == 2 + j, p_hi[:, j : j + 1], 0.0)
            b = b + jnp.where(row == 2 + j, p_lo[:, j : j + 1], 0.0)
        out[h, PART : PART + 16, 0:D] = a.astype(BF16)
        out[h, PART : PART + 16, D : 2 * D] = b.astype(BF16)
        out[h, PART : PART + 16, 2 * D : 3 * D] = c.astype(BF16)


def homes(y):
    return [y, (y + 3) % YS, (y + 1) % YS, (y + 2) % YS]


def column(a, r):
    return jnp.concatenate([a[:, 2 * r : 2 * r + 1], a[:, 2 * r + 1 : 2 * r + 2]], axis=0)


def paired(w, first, last):
    _, _, y_at, core = place()
    return [
        jnp.concatenate([w[2 * y + core, 0:LEN, first:last], w[2 * y + 1 - core, 0:LEN, first:last]], axis=0)
        for y in homes(y_at)
    ]


def encoded_dot(mine, theirs, pairs, lo, size):
    acc = None
    for i in range(4):
        k, at = (i, lo) if i < 3 else (3, lo) if lo < BLOCK // 2 else (4, lo - BLOCK // 2)
        both = jnp.concatenate([mine[k][at : at + size], theirs[k][at : at + size]], axis=1)
        term = jnp.dot(both, pairs[i], preferred_element_type=F32)
        acc = term if acc is None else acc + term
    return acc


def project_kernel(wait, part, *refs):
    mine, theirs = refs[0:5], refs[5:10]
    packet, cum_out, mask_out = refs[10:13]
    gates, places = refs[13:15]
    for c in range(NCH):
        info = part[c, PART : PART + 16, :].astype(F32)
        for p in range(3):
            gates[p, c : c + 1, :] = info[0:1, p * D : (p + 1) * D]
        mask_out[c : c + 1, :] = info[1:2, 0:D]
        for j in range(K):
            places[j * NCH + c : j * NCH + c + 1, :] = info[2 + j : 3 + j, 0:D] * 32.0 + info[2 + j : 3 + j, D : 2 * D]
    tri = (
        lax.broadcasted_iota(jnp.int32, (LEN, LEN), 0) <= lax.broadcasted_iota(jnp.int32, (LEN, LEN), 1)
    ).astype(BF16)
    cum = sum(jnp.dot(gates[p].astype(BF16), tri, preferred_element_type=F32) for p in range(3))
    rows, offset = [], jnp.zeros((1, 1), F32)
    for c in range(NCH):
        rows.append(cum[c : c + 1] + offset)
        offset = rows[-1][:, LEN - 1 : LEN]
    cum = jnp.concatenate(rows, axis=0)
    total = offset
    cum_out[...] = cum
    tail_t = jnp.exp(total - cum).T
    mask_t = mask_out[...].T
    pairs = paired(part, D, 3 * D)
    wait()
    state = jnp.zeros((D, D), F32)
    size = 256
    for r in range(BLOCK // size):
        lo = r * size
        acc = encoded_dot(mine, theirs, pairs, lo, size)
        keys = acc[:, 0:D].astype(BF16)
        values = (acc[:, D:].astype(BF16).astype(F32) * column(mask_t, r)).astype(BF16)
        scaled = (keys.astype(F32) * column(tail_t, r)).astype(BF16)
        state += lax.dot_general(scaled, values, (((0,), (0,)), ((), ())), preferred_element_type=F32)
    hot = (places[:, 0:1].astype(jnp.int32) == lax.broadcasted_iota(jnp.int32, (K * NCH, BLOCK), 1)).astype(F32)
    picked = jnp.dot(hot.astype(BF16), mine[0][...], preferred_element_type=F32).astype(BF16)
    row = lax.broadcasted_iota(jnp.int32, (16, D), 0)
    hi, mid, low = split3(total)
    info = (jnp.where(row == 0, hi, 0.0) + jnp.where(row == 1, mid, 0.0) + jnp.where(row == 2, low, 0.0)).astype(BF16)
    state = state.astype(BF16)
    for z in range(ZS):
        packet[z, 0:D, :] = state
        packet[z, D : D + 16, :] = info
        packet[z, D + 16 : D + 16 + K * NCH, :] = picked


FAR = K * ROW


def intra_kernel(wait, part, *refs):
    mine, theirs = refs[0:5], refs[5:10]
    cum, masks = refs[10:12]
    q, out, window, halo = refs[12:16]
    pairs = paired(part, 0, 3 * D)
    mask_t = masks[...].T
    wait()
    k, v = [], []
    size = 256
    cum_rows = cum[...]
    cum_t = cum_rows.T
    lower = lax.broadcasted_iota(jnp.int32, (size, size), 0) >= lax.broadcasted_iota(jnp.int32, (size, size), 1)
    for r in range(BLOCK // size):
        here = column(cum_t, r)
        acc = encoded_dot(mine, theirs, pairs, r * size, size)
        queries = acc[:, 0:D].astype(BF16)
        k.append(acc[:, D : 2 * D].astype(BF16))
        v.append((acc[:, 2 * D :].astype(BF16).astype(F32) * column(mask_t, r)).astype(BF16))
        q[r * size : (r + 1) * size] = queries
        acc = jnp.zeros((size, D), F32)
        for s in range(r + 1):
            diff = here - jnp.concatenate([cum_rows[2 * s : 2 * s + 1], cum_rows[2 * s + 1 : 2 * s + 2]], axis=1)
            if s == r:
                diff = jnp.where(lower, diff, -jnp.inf)
            scores = lax.dot_general(
                queries, k[s], (((1,), (1,)), ((), ())), preferred_element_type=F32
            )
            acc += jnp.dot((scores * jnp.exp(diff)).astype(BF16), v[s], preferred_element_type=F32)
        out[r * size : (r + 1) * size] = acc
    _, _, y_at, core = place()
    ys = homes(y_at)
    for b in range(3):
        at_row = 2 * y_at + core + b
        inside = jnp.minimum(at_row, NCH - 1)
        low = pl.ds(pl.multiple_of(jnp.minimum(inside, 3) * LEN, LEN), LEN)
        high = pl.ds(pl.multiple_of(jnp.maximum(inside - 4, 0) * LEN, LEN), LEN)
        rows = pl.ds(pl.multiple_of(inside * LEN, LEN), LEN)
        for i, y in enumerate(ys):
            for who, group in ((core, mine), (1 - core, theirs)):
                lanes = pl.ds(pl.multiple_of((2 * y + who) * D, D), D)
                if i < 3:
                    window[b * LEN : (b + 1) * LEN, lanes] = group[i][rows, :]
                else:
                    window[b * LEN : (b + 1) * LEN, lanes] = jnp.where(inside < 4, group[3][low, :], group[4][high, :])
    for i, y in enumerate(ys):
        for who, group in ((core, mine), (1 - core, theirs)):
            halo[pl.ds(pl.multiple_of((2 * y + who) * FAR, FAR), FAR), :] = group[i][0:FAR, :]
    row = lax.broadcasted_iota(jnp.int32, (16, D), 0)
    halo[NCH * FAR : NCH * FAR + 16, :] = (
        jnp.where(row == 0, masks[0:1], 0.0) + jnp.where(row == 1, masks[1:2], 0.0)
    ).astype(BF16)


def log_of(block):
    info = block.astype(F32)
    return info[0:1] + info[1:2] + info[2:3]


def row_kernel(z_in, packet, here_out, before_out):
    z_at = place()[1]
    row_state, here = jnp.zeros((D, D), F32), jnp.zeros((D, D), F32)
    row_log, before = jnp.zeros((1, D), F32), jnp.zeros((1, D), F32)
    for z in range(ZS):
        log = log_of(z_in[z, D : D + 16, :])
        factor, state = jnp.exp(log), z_in[z, 0:D, :].astype(F32)
        row_state = row_state * factor + state
        row_log = row_log + log
        here = jnp.where(z < z_at, here * factor + state, here)
        before = jnp.where(z < z_at, before + log, before)
    here_out[...] = here
    before_out[...] = jnp.broadcast_to(before, (8, D))
    row = lax.broadcasted_iota(jnp.int32, (16, D), 0)
    hi, mid, low = split3(row_log)
    info = (jnp.where(row == 0, hi, 0.0) + jnp.where(row == 1, mid, 0.0) + jnp.where(row == 2, low, 0.0)).astype(BF16)
    row_state = row_state.astype(BF16)
    n = K * NCH
    for x in range(XS):
        packet[x, 0:D, :] = row_state
        packet[x, D : D + 16, :] = info
        for z in range(ZS):
            packet[x, D + 16 + z * n : D + 16 + (z + 1) * n, :] = z_in[z, D + 16 : D + 16 + n, :]


def finish_kernel(wait, x_in, here, before, q, intra, cum, gain, out):
    x_at = place()[0]
    state = jnp.zeros((D, D), F32)
    for x in range(XS):
        log = log_of(x_in[x, D : D + 16, :])
        state = jnp.where(x < x_at, state * jnp.exp(log) + x_in[x, 0:D, :].astype(F32), state)
    incoming = (state * jnp.exp(before[0:1]) + here[...]).astype(BF16)
    wait()
    grow_t = jnp.exp(cum[...]).T
    scale = gain[:, pl.ds(pl.multiple_of(lax.axis_index("ch") * D, D), D)]
    size = 256
    for r in range(BLOCK // size):
        grow = jnp.concatenate([grow_t[:, 2 * r : 2 * r + 1], grow_t[:, 2 * r + 1 : 2 * r + 2]], axis=0)
        inter = jnp.dot(q[r * size : (r + 1) * size], incoming, preferred_element_type=F32)
        mixed = (intra[r * size : (r + 1) * size] + inter * grow) * D ** (-0.5)
        squares = jnp.mean(mixed * mixed, axis=-1, keepdims=True)
        context = (mixed / jnp.sqrt(squares + NORM_EPS) * scale).astype(BF16)
        out[2 * r] = context[0:LEN]
        out[2 * r + 1] = context[LEN:]


def predict_kernel(ctx, w, context, predicted, held, sems):
    copies = [pltpu.make_async_copy(w.at[j], held.at[j], sems.at[j]) for j in range(K)]
    for copy in copies:
        copy.start()
    whole = jnp.concatenate([ctx[h] for h in range(HEADS)], axis=1)
    context[...] = whole
    for j in range(K):
        copies[j].wait()
        predicted[j] = jnp.dot(whole, held[j], preferred_element_type=F32).astype(BF16)


def predict(ctx, w_pred):
    return pl.pallas_call(
        predict_kernel,
        out_shape=[shape((LEN, CIN), BF16), shape((K, LEN, CIN), BF16)],
        in_specs=[VMEM, HBM],
        out_specs=[VMEM, VMEM],
        scratch_shapes=[pltpu.VMEM((K, CIN, CIN), BF16), pltpu.SemaphoreType.DMA((K,))],
        name="predict",
        compiler_params=pltpu.CompilerParams(vmem_limit_bytes=GRANT),
        cost_estimate=pl.CostEstimate(flops=K * 2 * LEN * CIN * CIN, bytes_accessed=K * 2 * CIN * CIN, transcendentals=0),
    )(ctx, w_pred)


def loss_kernel(predicted, window, halo, masks, *refs):
    mine, theirs = refs[0:5], refs[5:10]
    loss, bank, ahead = refs[10:13]
    _, _, y_at, core = place()
    half = BLOCK // 2
    for i, y in enumerate(homes(y_at)):
        for who, group in ((core, mine), (1 - core, theirs)):
            lanes = pl.ds(pl.multiple_of((2 * y + who) * D, D), D)
            if i < 3:
                bank[:, lanes] = group[i][...]
            else:
                bank[0:half, lanes] = group[3][...]
                bank[half:, lanes] = group[4][...]
    me = 2 * y_at + core
    next_rows = halo[NCH * FAR : NCH * FAR + 16, :].astype(F32)
    ahead[0:LEN, :] = window[0:LEN, :]
    flags = [masks[pl.ds(me, 1), :]]
    for b in (1, 2):
        beyond = jnp.maximum(me + b - NCH, 0)

        @pl.when(me + b < NCH)
        def _():
            ahead[b * LEN : (b + 1) * LEN, :] = window[b * LEN : (b + 1) * LEN, :]

        @pl.when(me + b >= NCH)
        def _():
            for c in range(NCH):
                rows = pl.ds(pl.multiple_of(c * FAR + beyond * LEN, LEN), LEN)
                ahead[b * LEN : (b + 1) * LEN, c * D : (c + 1) * D] = halo[rows, :]

        outer = jnp.where(beyond == 0, next_rows[0:1], next_rows[1:2])
        flags.append(jnp.where(me + b < NCH, masks[pl.ds(jnp.minimum(me + b, NCH - 1), 1), :], outer))
    m0, m1, m2 = flags
    valid = [
        m0 * jnp.concatenate([m0[:, ROW:], m1[:, :ROW]], axis=1),
        m0 * m1,
        m0 * jnp.concatenate([m1[:, ROW:], m2[:, :ROW]], axis=1),
        m0 * m2,
    ]
    n = NSEQ * NCH
    for j in range(K):
        part = predicted[j]
        logits = (
            lax.dot_general(bank[j * n : (j + 1) * n, :], part, (((1,), (1,)), ((), ())), preferred_element_type=F32)
            * SCORE_SCALE
        )
        negsum = jnp.sum(jnp.exp(logits), axis=0, keepdims=True)
        acc = jnp.zeros((LEN, D), F32)
        for c in range(NCH):
            target = ahead[(j + 1) * ROW : (j + 1) * ROW + LEN, c * D : (c + 1) * D]
            acc += part[:, c * D : (c + 1) * D].astype(F32) * target.astype(F32)
        positive = jnp.sum(acc.T, axis=0, keepdims=True) * SCORE_SCALE
        loss[j : j + 1, :] = valid[j] * (jnp.log(jnp.exp(positive) + negsum) - positive)


def step(features, w_qkv, log_gate, norm_gain, w_pred, patch_mask, neg_index):
    mine, theirs = spread(features)
    (packed,) = call(
        pack_kernel, [shape((HEADS, PART + 16, 3 * D), BF16)],
        [w_qkv, log_gate, patch_mask.reshape(1, -1), neg_index.T], grant=False,
    )
    w_part = exchange(packed, "ch")
    pieces = [w_part, *mine, *theirs]
    whole = shape((BLOCK, D), BF16)
    n = K * NCH
    packet, cumul, masks = call(
        project_kernel,
        [shape((ZS, D + 16 + n, D), BF16), shape((NCH, LEN), F32), shape((NCH, LEN), F32)],
        pieces, held=(1,),
        flops=2 * BLOCK * CIN * 2 * D,
        scratch=[pltpu.VMEM((3, NCH, LEN), F32), pltpu.VMEM((n, D), F32)],
    )
    z_in = exchange(packet, "seq", ALONG_Z)
    queries, intra, window, halo = call(
        intra_kernel,
        [whole, shape((BLOCK, D), F32), shape((LEN + FAR, CIN), BF16), shape((NCH * FAR + 16, D), BF16)],
        [*pieces, cumul, masks], held=(1,),
        flops=2 * BLOCK * (BLOCK + CIN) * D,
    )
    x_packet, here, before = call(
        row_kernel, [shape((XS, D + 16 + ZS * n, D), BF16), shape((D, D), F32), shape((8, D), F32)], [z_in],
        after=[intra],
    )
    x_packet, halo = lax.optimization_barrier((x_packet, halo))
    x_in = exchange(x_packet, "seq", ALONG_X)
    pairs = [((s + 1) * NCH + c, s * NCH + c) for s in range(NSEQ - 1) for c in (NCH - 2, NCH - 1)]
    halo = lax.ppermute(halo, BOTH, pairs)
    (context,) = call(
        finish_kernel, [shape((NCH, LEN, D), BF16)],
        [x_in, here, before, queries, intra, cumul, norm_gain.reshape(1, -1)], held=(3, 4, 6), flops=2 * BLOCK * D * D,
    )
    bank = x_in[:, D + 16 :].reshape(XS * ZS, K, NCH, D).transpose(1, 0, 2, 3).reshape(K * NSEQ * NCH, D)
    context = exchange(context, "ch")
    bank_mine, bank_theirs = spread(bank)
    context, predicted = predict(context, w_pred)
    (loss,) = call(
        loss_kernel, [shape((K, LEN), F32)], [predicted, window, halo, masks, *bank_mine, *bank_theirs],
        flops=K * 2 * LEN * CIN * 256,
        scratch=[pltpu.VMEM((K * NSEQ * NCH, CIN), BF16), pltpu.VMEM((LEN + FAR, CIN), BF16)],
    )
    return context, loss


def solution(mesh):
    placed = (
        P("seq", "ch"),
        P("ch", None),
        P(None, BOTH),
        P(),
        P(),
        P(BOTH),
        P(None, BOTH),
    )
    return jax.shard_map(
        lambda *a: tuple(step(*a)),
        mesh=mesh,
        in_specs=placed,
        out_specs=(P(BOTH, None), P(None, BOTH)),
        check_vma=False,
    )
```

```python
import jax
import jax.numpy as jnp
from jax import lax
from jax.experimental import pallas as pl
from jax.experimental.pallas import tpu as pltpu
from jax.sharding import PartitionSpec as P


CIN = 1024
HEADS = 8
D = 128
K = 4
ROW = 64
NORM_EPS = 1e-06
XS, ZS, YS = 4, 8, 4
NSEQ, NCH = XS * ZS, 2 * YS
LEN = 128
BLOCK = NCH * LEN
F32 = jnp.float32
BF16 = jnp.bfloat16
BOTH = ("seq", "ch")
ALONG_Z = [[x * ZS + z for z in range(ZS)] for x in range(XS)]
ALONG_X = [[x * ZS + z for x in range(XS)] for z in range(ZS)]
GRANT = 24 * 1024 * 1024
SCORE_SCALE = 4.0 * CIN ** (-0.5)


def call(body, out, ins, flops=0, scratch=(), after=(), away=(), grant=True):
    n = len(ins)
    away = (*away, *range(n, n + len(after)))

    def kernel(*refs):
        body(*refs[:n], *refs[n + len(after) :])

    moved = sum(a.size * a.dtype.itemsize for a in ins) + sum(o.size * o.dtype.itemsize for o in out)
    return pl.pallas_call(
        kernel,
        out_shape=out,
        in_specs=[pl.BlockSpec(memory_space=pl.ANY) if i in away else pl.BlockSpec() for i in range(n + len(after))],
        out_specs=[pl.BlockSpec()] * len(out),
        scratch_shapes=list(scratch),
        cost_estimate=pl.CostEstimate(flops=flops, bytes_accessed=moved, transcendentals=0),
        compiler_params=pltpu.CompilerParams(vmem_limit_bytes=GRANT) if grant else None,
    )(*ins, *after)


def place():
    s, c = lax.axis_index("seq"), lax.axis_index("ch")
    return s >> 3, s & (ZS - 1), c >> 1, c & 1


def shape(dims, dtype):
    return jax.ShapeDtypeStruct(dims, dtype)


def exchange(x, axis, groups=None):
    return lax.all_to_all(x, axis, split_axis=0, concat_axis=0, axis_index_groups=groups)


def hop(x, dy, swap=False):
    pairs = []
    for c in range(NCH):
        y, k = c // 2, c % 2
        pairs.append((c, ((y + dy) % YS) * 2 + ((1 - k) if swap else k)))
    return lax.ppermute(x, "ch", pairs)


def spread(x):
    half = x.shape[0] // 2
    up, dn = hop(x, 1), hop(x, -1)
    other = hop(x, 0, True)
    far_a, far_b = hop(up[:half], 1), hop(dn[half:], -1)
    return [x, up, dn, far_a, far_b], [other] + [hop(a, 0, True) for a in (up, dn, far_a, far_b)]


def split3(x):
    hi = x.astype(BF16).astype(F32)
    mid = (x - hi).astype(BF16).astype(F32)
    return hi, mid, x - hi - mid


PART = LEN


def pack_kernel(w, gate, mask, neg, out):
    hi, mid, lo = split3(gate[...])
    m = mask[...].astype(F32)
    spot = neg[...] - lax.axis_index("seq") * BLOCK
    p_hi, p_lo = (spot >> 5).astype(F32), (spot & 31).astype(F32)
    row = lax.broadcasted_iota(jnp.int32, (16, LEN), 0)
    mine = w[...]
    for h in range(HEADS):
        for part in range(3):
            out[h, 0:PART, part * D : (part + 1) * D] = mine[:, (part * HEADS + h) * D : (part * HEADS + h + 1) * D]
        a = jnp.where(row == 0, hi[h : h + 1], 0.0) + jnp.where(row == 1, m, 0.0)
        b = jnp.where(row == 0, mid[h : h + 1], 0.0)
        c = jnp.where(row == 0, lo[h : h + 1], 0.0)
        for j in range(K):
            a = a + jnp.where(row == 2 + j, p_hi[:, j : j + 1], 0.0)
            b = b + jnp.where(row == 2 + j, p_lo[:, j : j + 1], 0.0)
        out[h, PART : PART + 16, 0:D] = a.astype(BF16)
        out[h, PART : PART + 16, D : 2 * D] = b.astype(BF16)
        out[h, PART : PART + 16, 2 * D : 3 * D] = c.astype(BF16)


def homes(y):
    return [y, (y + 3) % YS, (y + 1) % YS, (y + 2) % YS]


def column(a, r):
    return jnp.concatenate([a[:, 2 * r : 2 * r + 1], a[:, 2 * r + 1 : 2 * r + 2]], axis=0)


def paired(w, first, last):
    _, _, y_at, core = place()
    return [
        jnp.concatenate([w[2 * y + core, 0:LEN, first:last], w[2 * y + 1 - core, 0:LEN, first:last]], axis=0)
        for y in homes(y_at)
    ]


def encoded_dot(mine, theirs, pairs, lo, size):
    acc = None
    for i in range(4):
        k, at = (i, lo) if i < 3 else (3, lo) if lo < BLOCK // 2 else (4, lo - BLOCK // 2)
        both = jnp.concatenate([mine[k][at : at + size], theirs[k][at : at + size]], axis=1)
        term = jnp.dot(both, pairs[i], preferred_element_type=F32)
        acc = term if acc is None else acc + term
    return acc


def project_kernel(part, *refs):
    mine, theirs = refs[0:5], refs[5:10]
    packet, cum_out, mask_out = refs[10:13]
    gates, places = refs[13:15]
    for c in range(NCH):
        info = part[c, PART : PART + 16, :].astype(F32)
        for p in range(3):
            gates[p, c : c + 1, :] = info[0:1, p * D : (p + 1) * D]
        mask_out[c : c + 1, :] = info[1:2, 0:D]
        for j in range(K):
            places[j * NCH + c : j * NCH + c + 1, :] = info[2 + j : 3 + j, 0:D] * 32.0 + info[2 + j : 3 + j, D : 2 * D]
    tri = (
        lax.broadcasted_iota(jnp.int32, (LEN, LEN), 0) <= lax.broadcasted_iota(jnp.int32, (LEN, LEN), 1)
    ).astype(BF16)
    cum = sum(jnp.dot(gates[p].astype(BF16), tri, preferred_element_type=F32) for p in range(3))
    rows, offset = [], jnp.zeros((1, 1), F32)
    for c in range(NCH):
        rows.append(cum[c : c + 1] + offset)
        offset = rows[-1][:, LEN - 1 : LEN]
    cum = jnp.concatenate(rows, axis=0)
    total = offset
    cum_out[...] = cum
    tail_t = jnp.exp(total - cum).T
    mask_t = mask_out[...].T
    pairs = paired(part, D, 3 * D)
    state = jnp.zeros((D, D), F32)
    size = 256
    for r in range(BLOCK // size):
        lo = r * size
        acc = encoded_dot(mine, theirs, pairs, lo, size)
        keys = acc[:, 0:D].astype(BF16)
        values = (acc[:, D:].astype(BF16).astype(F32) * column(mask_t, r)).astype(BF16)
        scaled = (keys.astype(F32) * column(tail_t, r)).astype(BF16)
        state += lax.dot_general(scaled, values, (((0,), (0,)), ((), ())), preferred_element_type=F32)
    hot = (places[:, 0:1].astype(jnp.int32) == lax.broadcasted_iota(jnp.int32, (K * NCH, BLOCK), 1)).astype(F32)
    picked = jnp.dot(hot.astype(BF16), mine[0][...], preferred_element_type=F32).astype(BF16)
    row = lax.broadcasted_iota(jnp.int32, (16, D), 0)
    hi, mid, low = split3(total)
    info = (jnp.where(row == 0, hi, 0.0) + jnp.where(row == 1, mid, 0.0) + jnp.where(row == 2, low, 0.0)).astype(BF16)
    state = state.astype(BF16)
    for z in range(ZS):
        packet[z, 0:D, :] = state
        packet[z, D : D + 16, :] = info
        packet[z, D + 16 : D + 16 + K * NCH, :] = picked


FAR = K * ROW


def intra_kernel(part, *refs):
    mine, theirs = refs[0:5], refs[5:10]
    cum, masks = refs[10:12]
    q, out, window, halo = refs[12:16]
    pairs = paired(part, 0, 3 * D)
    mask_t = masks[...].T
    k, v = [], []
    size = 256
    cum_rows = cum[...]
    cum_t = cum_rows.T
    lower = lax.broadcasted_iota(jnp.int32, (size, size), 0) >= lax.broadcasted_iota(jnp.int32, (size, size), 1)
    for r in range(BLOCK // size):
        here = column(cum_t, r)
        acc = encoded_dot(mine, theirs, pairs, r * size, size)
        queries = acc[:, 0:D].astype(BF16)
        k.append(acc[:, D : 2 * D].astype(BF16))
        v.append((acc[:, 2 * D :].astype(BF16).astype(F32) * column(mask_t, r)).astype(BF16))
        q[r * size : (r + 1) * size] = queries
        acc = jnp.zeros((size, D), F32)
        for s in range(r + 1):
            diff = here - jnp.concatenate([cum_rows[2 * s : 2 * s + 1], cum_rows[2 * s + 1 : 2 * s + 2]], axis=1)
            if s == r:
                diff = jnp.where(lower, diff, -jnp.inf)
            scores = lax.dot_general(
                queries, k[s], (((1,), (1,)), ((), ())), preferred_element_type=F32
            )
            acc += jnp.dot((scores * jnp.exp(diff)).astype(BF16), v[s], preferred_element_type=F32)
        out[r * size : (r + 1) * size] = acc
    _, _, y_at, core = place()
    ys = homes(y_at)
    for b in range(3):
        at_row = 2 * y_at + core + b
        inside = jnp.minimum(at_row, NCH - 1)
        low = pl.ds(pl.multiple_of(jnp.minimum(inside, 3) * LEN, LEN), LEN)
        high = pl.ds(pl.multiple_of(jnp.maximum(inside - 4, 0) * LEN, LEN), LEN)
        rows = pl.ds(pl.multiple_of(inside * LEN, LEN), LEN)
        for i, y in enumerate(ys):
            for who, group in ((core, mine), (1 - core, theirs)):
                lanes = pl.ds(pl.multiple_of((2 * y + who) * D, D), D)
                if i < 3:
                    window[b * LEN : (b + 1) * LEN, lanes] = group[i][rows, :]
                else:
                    window[b * LEN : (b + 1) * LEN, lanes] = jnp.where(inside < 4, group[3][low, :], group[4][high, :])
    for i, y in enumerate(ys):
        for who, group in ((core, mine), (1 - core, theirs)):
            halo[pl.ds(pl.multiple_of((2 * y + who) * FAR, FAR), FAR), :] = group[i][0:FAR, :]
    row = lax.broadcasted_iota(jnp.int32, (16, D), 0)
    halo[NCH * FAR : NCH * FAR + 16, :] = (
        jnp.where(row == 0, masks[0:1], 0.0) + jnp.where(row == 1, masks[1:2], 0.0)
    ).astype(BF16)


def log_of(block):
    info = block.astype(F32)
    return info[0:1] + info[1:2] + info[2:3]


def row_kernel(z_in, packet, here_out, before_out):
    z_at = place()[1]
    row_state, here = jnp.zeros((D, D), F32), jnp.zeros((D, D), F32)
    row_log, before = jnp.zeros((1, D), F32), jnp.zeros((1, D), F32)
    for z in range(ZS):
        log = log_of(z_in[z, D : D + 16, :])
        factor, state = jnp.exp(log), z_in[z, 0:D, :].astype(F32)
        row_state = row_state * factor + state
        row_log = row_log + log
        here = jnp.where(z < z_at, here * factor + state, here)
        before = jnp.where(z < z_at, before + log, before)
    here_out[...] = here
    before_out[...] = jnp.broadcast_to(before, (8, D))
    row = lax.broadcasted_iota(jnp.int32, (16, D), 0)
    hi, mid, low = split3(row_log)
    info = (jnp.where(row == 0, hi, 0.0) + jnp.where(row == 1, mid, 0.0) + jnp.where(row == 2, low, 0.0)).astype(BF16)
    row_state = row_state.astype(BF16)
    n = K * NCH
    for x in range(XS):
        packet[x, 0:D, :] = row_state
        packet[x, D : D + 16, :] = info
        for z in range(ZS):
            packet[x, D + 16 + z * n : D + 16 + (z + 1) * n, :] = z_in[z, D + 16 : D + 16 + n, :]


def finish_kernel(x_in, here, before, q, intra, cum, gain, out):
    x_at = place()[0]
    state = jnp.zeros((D, D), F32)
    for x in range(XS):
        log = log_of(x_in[x, D : D + 16, :])
        state = jnp.where(x < x_at, state * jnp.exp(log) + x_in[x, 0:D, :].astype(F32), state)
    incoming = (state * jnp.exp(before[0:1]) + here[...]).astype(BF16)
    grow_t = jnp.exp(cum[...]).T
    scale = gain[:, pl.ds(pl.multiple_of(lax.axis_index("ch") * D, D), D)]
    size = 256
    for r in range(BLOCK // size):
        grow = jnp.concatenate([grow_t[:, 2 * r : 2 * r + 1], grow_t[:, 2 * r + 1 : 2 * r + 2]], axis=0)
        inter = jnp.dot(q[r * size : (r + 1) * size], incoming, preferred_element_type=F32)
        mixed = (intra[r * size : (r + 1) * size] + inter * grow) * D ** (-0.5)
        squares = jnp.mean(mixed * mixed, axis=-1, keepdims=True)
        context = (mixed / jnp.sqrt(squares + NORM_EPS) * scale).astype(BF16)
        out[2 * r] = context[0:LEN]
        out[2 * r + 1] = context[LEN:]


def predict_kernel(ctx, w, context, predicted):
    whole = jnp.concatenate([ctx[h] for h in range(HEADS)], axis=1)
    context[...] = whole
    for j in range(K):
        predicted[j] = jnp.dot(whole, w[j], preferred_element_type=F32).astype(BF16)


def loss_kernel(predicted, window, halo_far, masks, *refs):
    mine, theirs = refs[0:5], refs[5:10]
    loss, ahead, halo, sem = refs[10:14]
    arrival = pltpu.make_async_copy(halo_far, halo, sem)
    arrival.start()
    _, _, y_at, core = place()
    n = NSEQ * NCH
    negsums = []
    for j in range(K):
        logits = jnp.zeros((n, LEN), F32)
        for i, y in enumerate(homes(y_at)):
            k, lo = (i, j * n) if i < 3 else (3, j * n) if j < K // 2 else (4, (j - K // 2) * n)
            both = jnp.concatenate([mine[k][lo : lo + n], theirs[k][lo : lo + n]], axis=1)
            lanes = [pl.ds(pl.multiple_of((2 * y + who) * D, D), D) for who in (core, 1 - core)]
            part = jnp.concatenate([predicted[j, :, lanes[0]], predicted[j, :, lanes[1]]], axis=1)
            logits += lax.dot_general(both, part, (((1,), (1,)), ((), ())), preferred_element_type=F32)
        negsums.append(jnp.sum(jnp.exp(logits * SCORE_SCALE), axis=0, keepdims=True))
    me = 2 * y_at + core
    arrival.wait()
    next_rows = halo[NCH * FAR : NCH * FAR + 16, :].astype(F32)
    ahead[0:LEN, :] = window[0:LEN, :]
    flags = [masks[pl.ds(me, 1), :]]
    for b in (1, 2):
        beyond = jnp.maximum(me + b - NCH, 0)

        @pl.when(me + b < NCH)
        def _():
            ahead[b * LEN : (b + 1) * LEN, :] = window[b * LEN : (b + 1) * LEN, :]

        @pl.when(me + b >= NCH)
        def _():
            for c in range(NCH):
                rows = pl.ds(pl.multiple_of(c * FAR + beyond * LEN, LEN), LEN)
                ahead[b * LEN : (b + 1) * LEN, c * D : (c + 1) * D] = halo[rows, :]

        outer = jnp.where(beyond == 0, next_rows[0:1], next_rows[1:2])
        flags.append(jnp.where(me + b < NCH, masks[pl.ds(jnp.minimum(me + b, NCH - 1), 1), :], outer))
    m0, m1, m2 = flags
    valid = [
        m0 * jnp.concatenate([m0[:, ROW:], m1[:, :ROW]], axis=1),
        m0 * m1,
        m0 * jnp.concatenate([m1[:, ROW:], m2[:, :ROW]], axis=1),
        m0 * m2,
    ]
    for j in range(K):
        part = predicted[j]
        acc = jnp.zeros((LEN, D), F32)
        for c in range(NCH):
            target = ahead[(j + 1) * ROW : (j + 1) * ROW + LEN, c * D : (c + 1) * D]
            acc += part[:, c * D : (c + 1) * D].astype(F32) * target.astype(F32)
        positive = jnp.sum(acc.T, axis=0, keepdims=True) * SCORE_SCALE
        loss[j : j + 1, :] = valid[j] * (jnp.log(jnp.exp(positive) + negsums[j]) - positive)


def step(features, w_qkv, log_gate, norm_gain, w_pred, patch_mask, neg_index):
    mine, theirs = spread(features)
    (packed,) = call(
        pack_kernel, [shape((HEADS, PART + 16, 3 * D), BF16)],
        [w_qkv, log_gate, patch_mask.reshape(1, -1), neg_index.T], grant=False,
    )
    w_part = exchange(packed, "ch")
    pieces = [w_part, *mine, *theirs]
    whole = shape((BLOCK, D), BF16)
    n = K * NCH
    packet, cumul, masks = call(
        project_kernel,
        [shape((ZS, D + 16 + n, D), BF16), shape((NCH, LEN), F32), shape((NCH, LEN), F32)],
        pieces,
        flops=2 * BLOCK * CIN * 2 * D,
        scratch=[pltpu.VMEM((3, NCH, LEN), F32), pltpu.VMEM((n, D), F32)],
    )
    z_in = exchange(packet, "seq", ALONG_Z)
    queries, intra, window, halo = call(
        intra_kernel,
        [whole, shape((BLOCK, D), F32), shape((LEN + FAR, CIN), BF16), shape((NCH * FAR + 16, D), BF16)],
        [*pieces, cumul, masks],
        flops=2 * BLOCK * (BLOCK + CIN) * D,
    )
    x_packet, here, before = call(
        row_kernel, [shape((XS, D + 16 + ZS * n, D), BF16), shape((D, D), F32), shape((8, D), F32)], [z_in],
        after=[intra, queries],
    )
    x_packet, halo = lax.optimization_barrier((x_packet, halo))
    x_in = exchange(x_packet, "seq", ALONG_X)
    pairs = [((s + 1) * NCH + c, s * NCH + c) for s in range(NSEQ - 1) for c in (NCH - 2, NCH - 1)]
    halo = lax.ppermute(halo, BOTH, pairs)
    (context,) = call(
        finish_kernel, [shape((NCH, LEN, D), BF16)],
        [x_in, here, before, queries, intra, cumul, norm_gain.reshape(1, -1)], flops=2 * BLOCK * D * D,
    )
    bank = x_in[:, D + 16 :].reshape(XS * ZS, K, NCH, D).transpose(1, 0, 2, 3).reshape(K * NSEQ * NCH, D)
    context = exchange(context, "ch")
    bank_mine, bank_theirs = spread(bank)
    context, predicted = call(
        predict_kernel, [shape((LEN, CIN), BF16), shape((K, LEN, CIN), BF16)], [context, w_pred],
        flops=K * 2 * LEN * CIN * CIN,
    )
    (loss,) = call(
        loss_kernel, [shape((K, LEN), F32)], [predicted, window, halo, masks, *bank_mine, *bank_theirs],
        away=(2,),
        flops=K * 2 * LEN * CIN * 256,
        scratch=[pltpu.VMEM((LEN + FAR, CIN), BF16), pltpu.VMEM(halo.shape, BF16), pltpu.SemaphoreType.DMA],
    )
    return context, loss


def solution(mesh):
    placed = (
        P("seq", "ch"),
        P("ch", None),
        P(None, BOTH),
        P(),
        P(),
        P(BOTH),
        P(None, BOTH),
    )
    return jax.shard_map(
        lambda *a: tuple(step(*a)),
        mesh=mesh,
        in_specs=placed,
        out_specs=(P(BOTH, None), P(None, BOTH)),
        check_vma=False,
    )
```

```python
import jax
import jax.numpy as jnp
from jax import lax
from jax.experimental import pallas as pl
from jax.experimental.pallas import tpu as pltpu
from jax.sharding import PartitionSpec as P


CIN = 1024
HEADS = 8
D = 128
K = 4
ROW = 64
NORM_EPS = 1e-06
XS, ZS, YS = 4, 8, 4
NSEQ, NCH = XS * ZS, 2 * YS
LEN = 128
BLOCK = NCH * LEN
F32 = jnp.float32
BF16 = jnp.bfloat16
BOTH = ("seq", "ch")
ALONG_Z = [[x * ZS + z for z in range(ZS)] for x in range(XS)]
ALONG_X = [[x * ZS + z for x in range(XS)] for z in range(ZS)]
GRANT = 24 * 1024 * 1024
SCORE_SCALE = 4.0 * CIN ** (-0.5)


def call(body, out, ins, flops=0, scratch=(), after=(), away=(), grant=True):
    n = len(ins)
    away = (*away, *range(n, n + len(after)))

    def kernel(*refs):
        body(*refs[:n], *refs[n + len(after) :])

    moved = sum(a.size * a.dtype.itemsize for a in ins) + sum(o.size * o.dtype.itemsize for o in out)
    return pl.pallas_call(
        kernel,
        out_shape=out,
        in_specs=[pl.BlockSpec(memory_space=pl.ANY) if i in away else pl.BlockSpec() for i in range(n + len(after))],
        out_specs=[pl.BlockSpec()] * len(out),
        scratch_shapes=list(scratch),
        cost_estimate=pl.CostEstimate(flops=flops, bytes_accessed=moved, transcendentals=0),
        compiler_params=pltpu.CompilerParams(vmem_limit_bytes=GRANT) if grant else None,
    )(*ins, *after)


def place():
    s, c = lax.axis_index("seq"), lax.axis_index("ch")
    return s >> 3, s & (ZS - 1), c >> 1, c & 1


def shape(dims, dtype):
    return jax.ShapeDtypeStruct(dims, dtype)


def exchange(x, axis, groups=None):
    return lax.all_to_all(x, axis, split_axis=0, concat_axis=0, axis_index_groups=groups)


def hop(x, dy, swap=False):
    pairs = []
    for c in range(NCH):
        y, k = c // 2, c % 2
        pairs.append((c, ((y + dy) % YS) * 2 + ((1 - k) if swap else k)))
    return lax.ppermute(x, "ch", pairs)


def spread(x, cut):
    up, dn = hop(x, 1), hop(x, -1)
    other = hop(x, 0, True)
    far_a, far_b = hop(up[:cut], 1), hop(dn[cut:], -1)
    return [x, up, dn, far_a, far_b], [other] + [hop(a, 0, True) for a in (up, dn, far_a, far_b)]


def split3(x):
    hi = x.astype(BF16).astype(F32)
    mid = (x - hi).astype(BF16).astype(F32)
    return hi, mid, x - hi - mid


PART = LEN


def pack_kernel(w, gate, mask, neg, out):
    hi, mid, lo = split3(gate[...])
    m = mask[...].astype(F32)
    spot = neg[...] - lax.axis_index("seq") * BLOCK
    p_hi, p_lo = (spot >> 5).astype(F32), (spot & 31).astype(F32)
    row = lax.broadcasted_iota(jnp.int32, (16, LEN), 0)
    mine = w[...]
    for h in range(HEADS):
        for part in range(3):
            out[h, 0:PART, part * D : (part + 1) * D] = mine[:, (part * HEADS + h) * D : (part * HEADS + h + 1) * D]
        a = jnp.where(row == 0, hi[h : h + 1], 0.0) + jnp.where(row == 1, m, 0.0)
        b = jnp.where(row == 0, mid[h : h + 1], 0.0)
        c = jnp.where(row == 0, lo[h : h + 1], 0.0)
        for j in range(K):
            a = a + jnp.where(row == 2 + j, p_hi[:, j : j + 1], 0.0)
            b = b + jnp.where(row == 2 + j, p_lo[:, j : j + 1], 0.0)
        out[h, PART : PART + 16, 0:D] = a.astype(BF16)
        out[h, PART : PART + 16, D : 2 * D] = b.astype(BF16)
        out[h, PART : PART + 16, 2 * D : 3 * D] = c.astype(BF16)


def homes(y):
    return [y, (y + 3) % YS, (y + 1) % YS, (y + 2) % YS]


def column(a, r):
    return jnp.concatenate([a[:, 2 * r : 2 * r + 1], a[:, 2 * r + 1 : 2 * r + 2]], axis=0)


def paired(w, first, last):
    _, _, y_at, core = place()
    return [
        jnp.concatenate([w[2 * y + core, 0:LEN, first:last], w[2 * y + 1 - core, 0:LEN, first:last]], axis=0)
        for y in homes(y_at)
    ]


def encoded_dot(mine, theirs, pairs, lo, size):
    acc = None
    for i in range(4):
        k, at = (i, lo) if i < 3 else (3, lo) if lo < BLOCK // 2 else (4, lo - BLOCK // 2)
        both = jnp.concatenate([mine[k][at : at + size], theirs[k][at : at + size]], axis=1)
        term = jnp.dot(both, pairs[i], preferred_element_type=F32)
        acc = term if acc is None else acc + term
    return acc


def project_kernel(part, *refs):
    mine, theirs = refs[0:5], refs[5:10]
    packet, cum_out, mask_out = refs[10:13]
    gates, places = refs[13:15]
    for c in range(NCH):
        info = part[c, PART : PART + 16, :].astype(F32)
        for p in range(3):
            gates[p, c : c + 1, :] = info[0:1, p * D : (p + 1) * D]
        mask_out[c : c + 1, :] = info[1:2, 0:D]
        for j in range(K):
            places[j * NCH + c : j * NCH + c + 1, :] = info[2 + j : 3 + j, 0:D] * 32.0 + info[2 + j : 3 + j, D : 2 * D]
    tri = (
        lax.broadcasted_iota(jnp.int32, (LEN, LEN), 0) <= lax.broadcasted_iota(jnp.int32, (LEN, LEN), 1)
    ).astype(BF16)
    cum = sum(jnp.dot(gates[p].astype(BF16), tri, preferred_element_type=F32) for p in range(3))
    rows, offset = [], jnp.zeros((1, 1), F32)
    for c in range(NCH):
        rows.append(cum[c : c + 1] + offset)
        offset = rows[-1][:, LEN - 1 : LEN]
    cum = jnp.concatenate(rows, axis=0)
    total = offset
    cum_out[...] = cum
    tail_t = jnp.exp(total - cum).T
    mask_t = mask_out[...].T
    pairs = paired(part, D, 3 * D)
    state = jnp.zeros((D, D), F32)
    size = 256
    for r in range(BLOCK // size):
        lo = r * size
        acc = encoded_dot(mine, theirs, pairs, lo, size)
        keys = acc[:, 0:D].astype(BF16)
        values = (acc[:, D:].astype(BF16).astype(F32) * column(mask_t, r)).astype(BF16)
        scaled = (keys.astype(F32) * column(tail_t, r)).astype(BF16)
        state += lax.dot_general(scaled, values, (((0,), (0,)), ((), ())), preferred_element_type=F32)
    hot = (places[:, 0:1].astype(jnp.int32) == lax.broadcasted_iota(jnp.int32, (K * NCH, BLOCK), 1)).astype(F32)
    picked = jnp.dot(hot.astype(BF16), mine[0][...], preferred_element_type=F32).astype(BF16)
    row = lax.broadcasted_iota(jnp.int32, (16, D), 0)
    hi, mid, low = split3(total)
    info = (jnp.where(row == 0, hi, 0.0) + jnp.where(row == 1, mid, 0.0) + jnp.where(row == 2, low, 0.0)).astype(BF16)
    state = state.astype(BF16)
    for z in range(ZS):
        packet[z, 0:D, :] = state
        packet[z, D : D + 16, :] = info
        packet[z, D + 16 : D + 16 + K * NCH, :] = picked


FAR = K * ROW


def intra_kernel(part, *refs):
    mine, theirs = refs[0:5], refs[5:10]
    cum, masks = refs[10:12]
    q, out, window, halo = refs[12:16]
    pairs = paired(part, 0, 3 * D)
    mask_t = masks[...].T
    k, v = [], []
    size = 256
    cum_rows = cum[...]
    cum_t = cum_rows.T
    lower = lax.broadcasted_iota(jnp.int32, (size, size), 0) >= lax.broadcasted_iota(jnp.int32, (size, size), 1)
    for r in range(BLOCK // size):
        here = column(cum_t, r)
        acc = encoded_dot(mine, theirs, pairs, r * size, size)
        queries = acc[:, 0:D].astype(BF16)
        k.append(acc[:, D : 2 * D].astype(BF16))
        v.append((acc[:, 2 * D :].astype(BF16).astype(F32) * column(mask_t, r)).astype(BF16))
        q[r * size : (r + 1) * size] = queries
        acc = jnp.zeros((size, D), F32)
        for s in range(r + 1):
            diff = here - jnp.concatenate([cum_rows[2 * s : 2 * s + 1], cum_rows[2 * s + 1 : 2 * s + 2]], axis=1)
            if s == r:
                diff = jnp.where(lower, diff, -jnp.inf)
            scores = lax.dot_general(
                queries, k[s], (((1,), (1,)), ((), ())), preferred_element_type=F32
            )
            acc += jnp.dot((scores * jnp.exp(diff)).astype(BF16), v[s], preferred_element_type=F32)
        out[r * size : (r + 1) * size] = acc
    _, _, y_at, core = place()
    ys = homes(y_at)
    for b in range(3):
        at_row = 2 * y_at + core + b
        inside = jnp.minimum(at_row, NCH - 1)
        low = pl.ds(pl.multiple_of(jnp.minimum(inside, 3) * LEN, LEN), LEN)
        high = pl.ds(pl.multiple_of(jnp.maximum(inside - 4, 0) * LEN, LEN), LEN)
        rows = pl.ds(pl.multiple_of(inside * LEN, LEN), LEN)
        for i, y in enumerate(ys):
            for who, group in ((core, mine), (1 - core, theirs)):
                lanes = pl.ds(pl.multiple_of((2 * y + who) * D, D), D)
                if i < 3:
                    window[b * LEN : (b + 1) * LEN, lanes] = group[i][rows, :]
                else:
                    window[b * LEN : (b + 1) * LEN, lanes] = jnp.where(inside < 4, group[3][low, :], group[4][high, :])
    for i, y in enumerate(ys):
        for who, group in ((core, mine), (1 - core, theirs)):
            halo[pl.ds(pl.multiple_of((2 * y + who) * FAR, FAR), FAR), :] = group[i][0:FAR, :]
    row = lax.broadcasted_iota(jnp.int32, (16, D), 0)
    halo[NCH * FAR : NCH * FAR + 16, :] = (
        jnp.where(row == 0, masks[0:1], 0.0) + jnp.where(row == 1, masks[1:2], 0.0)
    ).astype(BF16)


def log_of(block):
    info = block.astype(F32)
    return info[0:1] + info[1:2] + info[2:3]


def row_kernel(z_in, packet, here_out, before_out):
    z_at = place()[1]
    row_state, here = jnp.zeros((D, D), F32), jnp.zeros((D, D), F32)
    row_log, before = jnp.zeros((1, D), F32), jnp.zeros((1, D), F32)
    for z in range(ZS):
        log = log_of(z_in[z, D : D + 16, :])
        factor, state = jnp.exp(log), z_in[z, 0:D, :].astype(F32)
        row_state = row_state * factor + state
        row_log = row_log + log
        here = jnp.where(z < z_at, here * factor + state, here)
        before = jnp.where(z < z_at, before + log, before)
    here_out[...] = here
    before_out[...] = jnp.broadcast_to(before, (8, D))
    row = lax.broadcasted_iota(jnp.int32, (16, D), 0)
    hi, mid, low = split3(row_log)
    info = (jnp.where(row == 0, hi, 0.0) + jnp.where(row == 1, mid, 0.0) + jnp.where(row == 2, low, 0.0)).astype(BF16)
    row_state = row_state.astype(BF16)
    n = K * NCH
    for x in range(XS):
        packet[x, 0:D, :] = row_state
        packet[x, D : D + 16, :] = info
        for z in range(ZS):
            packet[x, D + 16 + z * n : D + 16 + (z + 1) * n, :] = z_in[z, D + 16 : D + 16 + n, :]


def finish_kernel(x_in, here, before, q, intra, cum, gain, out):
    x_at = place()[0]
    state = jnp.zeros((D, D), F32)
    for x in range(XS):
        log = log_of(x_in[x, D : D + 16, :])
        state = jnp.where(x < x_at, state * jnp.exp(log) + x_in[x, 0:D, :].astype(F32), state)
    incoming = (state * jnp.exp(before[0:1]) + here[...]).astype(BF16)
    grow_t = jnp.exp(cum[...]).T
    scale = gain[:, pl.ds(pl.multiple_of(lax.axis_index("ch") * D, D), D)]
    size = 256
    for r in range(BLOCK // size):
        grow = jnp.concatenate([grow_t[:, 2 * r : 2 * r + 1], grow_t[:, 2 * r + 1 : 2 * r + 2]], axis=0)
        inter = jnp.dot(q[r * size : (r + 1) * size], incoming, preferred_element_type=F32)
        mixed = (intra[r * size : (r + 1) * size] + inter * grow) * D ** (-0.5)
        squares = jnp.mean(mixed * mixed, axis=-1, keepdims=True)
        context = (mixed / jnp.sqrt(squares + NORM_EPS) * scale).astype(BF16)
        out[2 * r] = context[0:LEN]
        out[2 * r + 1] = context[LEN:]


def predict_kernel(ctx, w, context, predicted):
    whole = jnp.concatenate([ctx[h] for h in range(HEADS)], axis=1)
    context[...] = whole
    for j in range(K):
        predicted[j] = jnp.dot(whole, w[j], preferred_element_type=F32).astype(BF16)


def loss_kernel(predicted, window, halo_far, masks, *refs):
    mine, theirs = refs[0:5], refs[5:10]
    loss, ahead, halo, sem = refs[10:14]
    arrival = pltpu.make_async_copy(halo_far, halo, sem)
    arrival.start()
    _, _, y_at, core = place()
    n = NSEQ * NCH
    negsums = []
    for j in range(K):
        logits = jnp.zeros((n, LEN), F32)
        for i, y in enumerate(homes(y_at)):
            k, lo = (i, j * n) if i < 3 else (3, 0) if j == 0 else (4, (j - 1) * n)
            both = jnp.concatenate([mine[k][lo : lo + n], theirs[k][lo : lo + n]], axis=1)
            lanes = [pl.ds(pl.multiple_of((2 * y + who) * D, D), D) for who in (core, 1 - core)]
            part = jnp.concatenate([predicted[j, :, lanes[0]], predicted[j, :, lanes[1]]], axis=1)
            logits += lax.dot_general(both, part, (((1,), (1,)), ((), ())), preferred_element_type=F32)
        negsums.append(jnp.sum(jnp.exp(logits * SCORE_SCALE), axis=0, keepdims=True))
    me = 2 * y_at + core
    arrival.wait()
    next_rows = halo[NCH * FAR : NCH * FAR + 16, :].astype(F32)
    ahead[0:LEN, :] = window[0:LEN, :]
    flags = [masks[pl.ds(me, 1), :]]
    for b in (1, 2):
        beyond = jnp.maximum(me + b - NCH, 0)

        @pl.when(me + b < NCH)
        def _():
            ahead[b * LEN : (b + 1) * LEN, :] = window[b * LEN : (b + 1) * LEN, :]

        @pl.when(me + b >= NCH)
        def _():
            for c in range(NCH):
                rows = pl.ds(pl.multiple_of(c * FAR + beyond * LEN, LEN), LEN)
                ahead[b * LEN : (b + 1) * LEN, c * D : (c + 1) * D] = halo[rows, :]

        outer = jnp.where(beyond == 0, next_rows[0:1], next_rows[1:2])
        flags.append(jnp.where(me + b < NCH, masks[pl.ds(jnp.minimum(me + b, NCH - 1), 1), :], outer))
    m0, m1, m2 = flags
    valid = [
        m0 * jnp.concatenate([m0[:, ROW:], m1[:, :ROW]], axis=1),
        m0 * m1,
        m0 * jnp.concatenate([m1[:, ROW:], m2[:, :ROW]], axis=1),
        m0 * m2,
    ]
    for j in range(K):
        part = predicted[j]
        acc = jnp.zeros((LEN, D), F32)
        for c in range(NCH):
            target = ahead[(j + 1) * ROW : (j + 1) * ROW + LEN, c * D : (c + 1) * D]
            acc += part[:, c * D : (c + 1) * D].astype(F32) * target.astype(F32)
        positive = jnp.sum(acc.T, axis=0, keepdims=True) * SCORE_SCALE
        loss[j : j + 1, :] = valid[j] * (jnp.log(jnp.exp(positive) + negsums[j]) - positive)


def step(features, w_qkv, log_gate, norm_gain, w_pred, patch_mask, neg_index):
    mine, theirs = spread(features, BLOCK // 2)
    (packed,) = call(
        pack_kernel, [shape((HEADS, PART + 16, 3 * D), BF16)],
        [w_qkv, log_gate, patch_mask.reshape(1, -1), neg_index.T], grant=False,
    )
    w_part = exchange(packed, "ch")
    pieces = [w_part, *mine, *theirs]
    whole = shape((BLOCK, D), BF16)
    n = K * NCH
    packet, cumul, masks = call(
        project_kernel,
        [shape((ZS, D + 16 + n, D), BF16), shape((NCH, LEN), F32), shape((NCH, LEN), F32)],
        pieces,
        flops=2 * BLOCK * CIN * 2 * D,
        scratch=[pltpu.VMEM((3, NCH, LEN), F32), pltpu.VMEM((n, D), F32)],
    )
    z_in = exchange(packet, "seq", ALONG_Z)
    queries, intra, window, halo = call(
        intra_kernel,
        [whole, shape((BLOCK, D), F32), shape((LEN + FAR, CIN), BF16), shape((NCH * FAR + 16, D), BF16)],
        [*pieces, cumul, masks],
        flops=2 * BLOCK * (BLOCK + CIN) * D,
    )
    x_packet, here, before = call(
        row_kernel, [shape((XS, D + 16 + ZS * n, D), BF16), shape((D, D), F32), shape((8, D), F32)], [z_in],
        after=[intra, queries],
    )
    x_packet, halo = lax.optimization_barrier((x_packet, halo))
    x_in = exchange(x_packet, "seq", ALONG_X)
    pairs = [((s + 1) * NCH + c, s * NCH + c) for s in range(NSEQ - 1) for c in (NCH - 2, NCH - 1)]
    halo = lax.ppermute(halo, BOTH, pairs)
    (context,) = call(
        finish_kernel, [shape((NCH, LEN, D), BF16)],
        [x_in, here, before, queries, intra, cumul, norm_gain.reshape(1, -1)], flops=2 * BLOCK * D * D,
    )
    bank = x_in[:, D + 16 :].reshape(XS * ZS, K, NCH, D).transpose(1, 0, 2, 3).reshape(K * NSEQ * NCH, D)
    context = exchange(context, "ch")
    bank_mine, bank_theirs = spread(bank, NSEQ * NCH)
    context, predicted = call(
        predict_kernel, [shape((LEN, CIN), BF16), shape((K, LEN, CIN), BF16)], [context, w_pred],
        flops=K * 2 * LEN * CIN * CIN,
    )
    (loss,) = call(
        loss_kernel, [shape((K, LEN), F32)], [predicted, window, halo, masks, *bank_mine, *bank_theirs],
        away=(2,),
        flops=K * 2 * LEN * CIN * 256,
        scratch=[pltpu.VMEM((LEN + FAR, CIN), BF16), pltpu.VMEM(halo.shape, BF16), pltpu.SemaphoreType.DMA],
    )
    return context, loss


def solution(mesh):
    placed = (
        P("seq", "ch"),
        P("ch", None),
        P(None, BOTH),
        P(),
        P(),
        P(BOTH),
        P(None, BOTH),
    )
    return jax.shard_map(
        lambda *a: tuple(step(*a)),
        mesh=mesh,
        in_specs=placed,
        out_specs=(P(BOTH, None), P(None, BOTH)),
        check_vma=False,
    )
```

```python
import jax
import jax.numpy as jnp
from jax import lax
from jax.experimental import pallas as pl
from jax.experimental.pallas import tpu as pltpu
from jax.sharding import PartitionSpec as P


CIN = 1024
HEADS = 8
D = 128
K = 4
ROW = 64
NORM_EPS = 1e-06
XS, ZS, YS = 4, 8, 4
NSEQ, NCH = XS * ZS, 2 * YS
LEN = 128
BLOCK = NCH * LEN
F32 = jnp.float32
BF16 = jnp.bfloat16
BOTH = ("seq", "ch")
ALONG_Z = [[x * ZS + z for z in range(ZS)] for x in range(XS)]
ALONG_X = [[x * ZS + z for x in range(XS)] for z in range(ZS)]
GRANT = 24 * 1024 * 1024
SCORE_SCALE = 4.0 * CIN ** (-0.5)


def call(body, out, ins, flops=0, scratch=(), after=(), away=(), grant=True):
    n = len(ins)
    away = (*away, *range(n, n + len(after)))

    def kernel(*refs):
        body(*refs[:n], *refs[n + len(after) :])

    moved = sum(a.size * a.dtype.itemsize for a in ins) + sum(o.size * o.dtype.itemsize for o in out)
    return pl.pallas_call(
        kernel,
        out_shape=out,
        in_specs=[pl.BlockSpec(memory_space=pl.ANY) if i in away else pl.BlockSpec() for i in range(n + len(after))],
        out_specs=[pl.BlockSpec()] * len(out),
        scratch_shapes=list(scratch),
        cost_estimate=pl.CostEstimate(flops=flops, bytes_accessed=moved, transcendentals=0),
        compiler_params=pltpu.CompilerParams(vmem_limit_bytes=GRANT) if grant else None,
    )(*ins, *after)


def place():
    s, c = lax.axis_index("seq"), lax.axis_index("ch")
    return s >> 3, s & (ZS - 1), c >> 1, c & 1


def shape(dims, dtype):
    return jax.ShapeDtypeStruct(dims, dtype)


def exchange(x, axis, groups=None):
    return lax.all_to_all(x, axis, split_axis=0, concat_axis=0, axis_index_groups=groups)


def hop(x, dy, swap=False):
    pairs = []
    for c in range(NCH):
        y, k = c // 2, c % 2
        pairs.append((c, ((y + dy) % YS) * 2 + ((1 - k) if swap else k)))
    return lax.ppermute(x, "ch", pairs)


def spread(x, cut):
    up, dn = hop(x, 1), hop(x, -1)
    other = hop(x, 0, True)
    far_a, far_b = hop(up[:cut], 1), hop(dn[cut:], -1)
    return [x, up, dn, far_a, far_b], [other] + [hop(a, 0, True) for a in (up, dn, far_a, far_b)]


def spread_down(x):
    up, dn = hop(x, 1), hop(x, -1)
    far = hop(dn, -1)
    return [x, up, dn, far], [hop(a, 0, True) for a in (x, up, dn, far)]


def split3(x):
    hi = x.astype(BF16).astype(F32)
    mid = (x - hi).astype(BF16).astype(F32)
    return hi, mid, x - hi - mid


PART = LEN


def pack_kernel(w, gate, mask, neg, out):
    hi, mid, lo = split3(gate[...])
    m = mask[...].astype(F32)
    spot = neg[...] - lax.axis_index("seq") * BLOCK
    p_hi, p_lo = (spot >> 5).astype(F32), (spot & 31).astype(F32)
    row = lax.broadcasted_iota(jnp.int32, (16, LEN), 0)
    mine = w[...]
    for h in range(HEADS):
        for part in range(3):
            out[h, 0:PART, part * D : (part + 1) * D] = mine[:, (part * HEADS + h) * D : (part * HEADS + h + 1) * D]
        a = jnp.where(row == 0, hi[h : h + 1], 0.0) + jnp.where(row == 1, m, 0.0)
        b = jnp.where(row == 0, mid[h : h + 1], 0.0)
        c = jnp.where(row == 0, lo[h : h + 1], 0.0)
        for j in range(K):
            a = a + jnp.where(row == 2 + j, p_hi[:, j : j + 1], 0.0)
            b = b + jnp.where(row == 2 + j, p_lo[:, j : j + 1], 0.0)
        out[h, PART : PART + 16, 0:D] = a.astype(BF16)
        out[h, PART : PART + 16, D : 2 * D] = b.astype(BF16)
        out[h, PART : PART + 16, 2 * D : 3 * D] = c.astype(BF16)


def homes(y):
    return [y, (y + 3) % YS, (y + 1) % YS, (y + 2) % YS]


def column(a, r):
    return jnp.concatenate([a[:, 2 * r : 2 * r + 1], a[:, 2 * r + 1 : 2 * r + 2]], axis=0)


def paired(w, first, last):
    _, _, y_at, core = place()
    return [
        jnp.concatenate([w[2 * y + core, 0:LEN, first:last], w[2 * y + 1 - core, 0:LEN, first:last]], axis=0)
        for y in homes(y_at)
    ]


def encoded_dot(mine, theirs, pairs, lo, size):
    acc = None
    for i in range(4):
        k, at = (i, lo) if i < 3 else (3, lo) if lo < BLOCK // 2 else (4, lo - BLOCK // 2)
        both = jnp.concatenate([mine[k][at : at + size], theirs[k][at : at + size]], axis=1)
        term = jnp.dot(both, pairs[i], preferred_element_type=F32)
        acc = term if acc is None else acc + term
    return acc


def project_kernel(part, *refs):
    mine, theirs = refs[0:5], refs[5:10]
    packet, cum_out, mask_out = refs[10:13]
    gates, places = refs[13:15]
    for c in range(NCH):
        info = part[c, PART : PART + 16, :].astype(F32)
        for p in range(3):
            gates[p, c : c + 1, :] = info[0:1, p * D : (p + 1) * D]
        mask_out[c : c + 1, :] = info[1:2, 0:D]
        for j in range(K):
            places[j * NCH + c : j * NCH + c + 1, :] = info[2 + j : 3 + j, 0:D] * 32.0 + info[2 + j : 3 + j, D : 2 * D]
    tri = (
        lax.broadcasted_iota(jnp.int32, (LEN, LEN), 0) <= lax.broadcasted_iota(jnp.int32, (LEN, LEN), 1)
    ).astype(BF16)
    cum = sum(jnp.dot(gates[p].astype(BF16), tri, preferred_element_type=F32) for p in range(3))
    rows, offset = [], jnp.zeros((1, 1), F32)
    for c in range(NCH):
        rows.append(cum[c : c + 1] + offset)
        offset = rows[-1][:, LEN - 1 : LEN]
    cum = jnp.concatenate(rows, axis=0)
    total = offset
    cum_out[...] = cum
    tail_t = jnp.exp(total - cum).T
    mask_t = mask_out[...].T
    pairs = paired(part, D, 3 * D)
    state = jnp.zeros((D, D), F32)
    size = 256
    for r in range(BLOCK // size):
        lo = r * size
        acc = encoded_dot(mine, theirs, pairs, lo, size)
        keys = acc[:, 0:D].astype(BF16)
        values = (acc[:, D:].astype(BF16).astype(F32) * column(mask_t, r)).astype(BF16)
        scaled = (keys.astype(F32) * column(tail_t, r)).astype(BF16)
        state += lax.dot_general(scaled, values, (((0,), (0,)), ((), ())), preferred_element_type=F32)
    hot = (places[:, 0:1].astype(jnp.int32) == lax.broadcasted_iota(jnp.int32, (K * NCH, BLOCK), 1)).astype(F32)
    picked = jnp.dot(hot.astype(BF16), mine[0][...], preferred_element_type=F32).astype(BF16)
    row = lax.broadcasted_iota(jnp.int32, (16, D), 0)
    hi, mid, low = split3(total)
    info = (jnp.where(row == 0, hi, 0.0) + jnp.where(row == 1, mid, 0.0) + jnp.where(row == 2, low, 0.0)).astype(BF16)
    state = state.astype(BF16)
    for z in range(ZS):
        packet[z, 0:D, :] = state
        packet[z, D : D + 16, :] = info
        packet[z, D + 16 : D + 16 + K * NCH, :] = picked


FAR = K * ROW


def intra_kernel(part, *refs):
    mine, theirs = refs[0:5], refs[5:10]
    cum, masks = refs[10:12]
    q, out, window, halo = refs[12:16]
    pairs = paired(part, 0, 3 * D)
    mask_t = masks[...].T
    k, v = [], []
    size = 256
    cum_rows = cum[...]
    cum_t = cum_rows.T
    lower = lax.broadcasted_iota(jnp.int32, (size, size), 0) >= lax.broadcasted_iota(jnp.int32, (size, size), 1)
    for r in range(BLOCK // size):
        here = column(cum_t, r)
        acc = encoded_dot(mine, theirs, pairs, r * size, size)
        queries = acc[:, 0:D].astype(BF16)
        k.append(acc[:, D : 2 * D].astype(BF16))
        v.append((acc[:, 2 * D :].astype(BF16).astype(F32) * column(mask_t, r)).astype(BF16))
        q[r * size : (r + 1) * size] = queries
        acc = jnp.zeros((size, D), F32)
        for s in range(r + 1):
            diff = here - jnp.concatenate([cum_rows[2 * s : 2 * s + 1], cum_rows[2 * s + 1 : 2 * s + 2]], axis=1)
            if s == r:
                diff = jnp.where(lower, diff, -jnp.inf)
            scores = lax.dot_general(
                queries, k[s], (((1,), (1,)), ((), ())), preferred_element_type=F32
            )
            acc += jnp.dot((scores * jnp.exp(diff)).astype(BF16), v[s], preferred_element_type=F32)
        out[r * size : (r + 1) * size] = acc
    _, _, y_at, core = place()
    ys = homes(y_at)
    for b in range(3):
        at_row = 2 * y_at + core + b
        inside = jnp.minimum(at_row, NCH - 1)
        low = pl.ds(pl.multiple_of(jnp.minimum(inside, 3) * LEN, LEN), LEN)
        high = pl.ds(pl.multiple_of(jnp.maximum(inside - 4, 0) * LEN, LEN), LEN)
        rows = pl.ds(pl.multiple_of(inside * LEN, LEN), LEN)
        for i, y in enumerate(ys):
            for who, group in ((core, mine), (1 - core, theirs)):
                lanes = pl.ds(pl.multiple_of((2 * y + who) * D, D), D)
                if i < 3:
                    window[b * LEN : (b + 1) * LEN, lanes] = group[i][rows, :]
                else:
                    window[b * LEN : (b + 1) * LEN, lanes] = jnp.where(inside < 4, group[3][low, :], group[4][high, :])
    for i, y in enumerate(ys):
        for who, group in ((core, mine), (1 - core, theirs)):
            halo[pl.ds(pl.multiple_of((2 * y + who) * FAR, FAR), FAR), :] = group[i][0:FAR, :]
    row = lax.broadcasted_iota(jnp.int32, (16, D), 0)
    halo[NCH * FAR : NCH * FAR + 16, :] = (
        jnp.where(row == 0, masks[0:1], 0.0) + jnp.where(row == 1, masks[1:2], 0.0)
    ).astype(BF16)


def log_of(block):
    info = block.astype(F32)
    return info[0:1] + info[1:2] + info[2:3]


def row_kernel(z_in, packet, here_out, before_out):
    z_at = place()[1]
    row_state, here = jnp.zeros((D, D), F32), jnp.zeros((D, D), F32)
    row_log, before = jnp.zeros((1, D), F32), jnp.zeros((1, D), F32)
    for z in range(ZS):
        log = log_of(z_in[z, D : D + 16, :])
        factor, state = jnp.exp(log), z_in[z, 0:D, :].astype(F32)
        row_state = row_state * factor + state
        row_log = row_log + log
        here = jnp.where(z < z_at, here * factor + state, here)
        before = jnp.where(z < z_at, before + log, before)
    here_out[...] = here
    before_out[...] = jnp.broadcast_to(before, (8, D))
    row = lax.broadcasted_iota(jnp.int32, (16, D), 0)
    hi, mid, low = split3(row_log)
    info = (jnp.where(row == 0, hi, 0.0) + jnp.where(row == 1, mid, 0.0) + jnp.where(row == 2, low, 0.0)).astype(BF16)
    row_state = row_state.astype(BF16)
    n = K * NCH
    for x in range(XS):
        packet[x, 0:D, :] = row_state
        packet[x, D : D + 16, :] = info
        for z in range(ZS):
            packet[x, D + 16 + z * n : D + 16 + (z + 1) * n, :] = z_in[z, D + 16 : D + 16 + n, :]


def finish_kernel(x_in, here, before, q, intra, cum, gain, out):
    x_at = place()[0]
    state = jnp.zeros((D, D), F32)
    for x in range(XS):
        log = log_of(x_in[x, D : D + 16, :])
        state = jnp.where(x < x_at, state * jnp.exp(log) + x_in[x, 0:D, :].astype(F32), state)
    incoming = (state * jnp.exp(before[0:1]) + here[...]).astype(BF16)
    grow_t = jnp.exp(cum[...]).T
    scale = gain[:, pl.ds(pl.multiple_of(lax.axis_index("ch") * D, D), D)]
    size = 256
    for r in range(BLOCK // size):
        grow = jnp.concatenate([grow_t[:, 2 * r : 2 * r + 1], grow_t[:, 2 * r + 1 : 2 * r + 2]], axis=0)
        inter = jnp.dot(q[r * size : (r + 1) * size], incoming, preferred_element_type=F32)
        mixed = (intra[r * size : (r + 1) * size] + inter * grow) * D ** (-0.5)
        squares = jnp.mean(mixed * mixed, axis=-1, keepdims=True)
        context = (mixed / jnp.sqrt(squares + NORM_EPS) * scale).astype(BF16)
        out[2 * r] = context[0:LEN]
        out[2 * r + 1] = context[LEN:]


def predict_kernel(ctx, w, context, predicted):
    whole = jnp.concatenate([ctx[h] for h in range(HEADS)], axis=1)
    context[...] = whole
    for j in range(K):
        predicted[j] = jnp.dot(whole, w[j], preferred_element_type=F32).astype(BF16)


def loss_kernel(predicted, window, halo_far, masks, *refs):
    mine, theirs = refs[0:4], refs[4:8]
    loss, ahead, halo, sem = refs[8:12]
    arrival = pltpu.make_async_copy(halo_far, halo, sem)
    arrival.start()
    _, _, y_at, core = place()
    n = NSEQ * NCH
    negsums = []
    for j in range(K):
        logits = jnp.zeros((n, LEN), F32)
        for i, y in enumerate(homes(y_at)):
            k, lo = i, j * n
            both = jnp.concatenate([mine[k][lo : lo + n], theirs[k][lo : lo + n]], axis=1)
            lanes = [pl.ds(pl.multiple_of((2 * y + who) * D, D), D) for who in (core, 1 - core)]
            part = jnp.concatenate([predicted[j, :, lanes[0]], predicted[j, :, lanes[1]]], axis=1)
            logits += lax.dot_general(both, part, (((1,), (1,)), ((), ())), preferred_element_type=F32)
        negsums.append(jnp.sum(jnp.exp(logits * SCORE_SCALE), axis=0, keepdims=True))
    me = 2 * y_at + core
    arrival.wait()
    next_rows = halo[NCH * FAR : NCH * FAR + 16, :].astype(F32)
    ahead[0:LEN, :] = window[0:LEN, :]
    flags = [masks[pl.ds(me, 1), :]]
    for b in (1, 2):
        beyond = jnp.maximum(me + b - NCH, 0)

        @pl.when(me + b < NCH)
        def _():
            ahead[b * LEN : (b + 1) * LEN, :] = window[b * LEN : (b + 1) * LEN, :]

        @pl.when(me + b >= NCH)
        def _():
            for c in range(NCH):
                rows = pl.ds(pl.multiple_of(c * FAR + beyond * LEN, LEN), LEN)
                ahead[b * LEN : (b + 1) * LEN, c * D : (c + 1) * D] = halo[rows, :]

        outer = jnp.where(beyond == 0, next_rows[0:1], next_rows[1:2])
        flags.append(jnp.where(me + b < NCH, masks[pl.ds(jnp.minimum(me + b, NCH - 1), 1), :], outer))
    m0, m1, m2 = flags
    valid = [
        m0 * jnp.concatenate([m0[:, ROW:], m1[:, :ROW]], axis=1),
        m0 * m1,
        m0 * jnp.concatenate([m1[:, ROW:], m2[:, :ROW]], axis=1),
        m0 * m2,
    ]
    for j in range(K):
        part = predicted[j]
        acc = jnp.zeros((LEN, D), F32)
        for c in range(NCH):
            target = ahead[(j + 1) * ROW : (j + 1) * ROW + LEN, c * D : (c + 1) * D]
            acc += part[:, c * D : (c + 1) * D].astype(F32) * target.astype(F32)
        positive = jnp.sum(acc.T, axis=0, keepdims=True) * SCORE_SCALE
        loss[j : j + 1, :] = valid[j] * (jnp.log(jnp.exp(positive) + negsums[j]) - positive)


def step(features, w_qkv, log_gate, norm_gain, w_pred, patch_mask, neg_index):
    mine, theirs = spread(features, BLOCK // 2)
    (packed,) = call(
        pack_kernel, [shape((HEADS, PART + 16, 3 * D), BF16)],
        [w_qkv, log_gate, patch_mask.reshape(1, -1), neg_index.T], grant=False,
    )
    w_part = exchange(packed, "ch")
    pieces = [w_part, *mine, *theirs]
    whole = shape((BLOCK, D), BF16)
    n = K * NCH
    packet, cumul, masks = call(
        project_kernel,
        [shape((ZS, D + 16 + n, D), BF16), shape((NCH, LEN), F32), shape((NCH, LEN), F32)],
        pieces,
        flops=2 * BLOCK * CIN * 2 * D,
        scratch=[pltpu.VMEM((3, NCH, LEN), F32), pltpu.VMEM((n, D), F32)],
    )
    z_in = exchange(packet, "seq", ALONG_Z)
    queries, intra, window, halo = call(
        intra_kernel,
        [whole, shape((BLOCK, D), F32), shape((LEN + FAR, CIN), BF16), shape((NCH * FAR + 16, D), BF16)],
        [*pieces, cumul, masks],
        flops=2 * BLOCK * (BLOCK + CIN) * D,
    )
    x_packet, here, before = call(
        row_kernel, [shape((XS, D + 16 + ZS * n, D), BF16), shape((D, D), F32), shape((8, D), F32)], [z_in],
        after=[intra, queries],
    )
    x_packet, halo = lax.optimization_barrier((x_packet, halo))
    x_in = exchange(x_packet, "seq", ALONG_X)
    pairs = [((s + 1) * NCH + c, s * NCH + c) for s in range(NSEQ - 1) for c in (NCH - 2, NCH - 1)]
    halo = lax.ppermute(halo, BOTH, pairs)
    (context,) = call(
        finish_kernel, [shape((NCH, LEN, D), BF16)],
        [x_in, here, before, queries, intra, cumul, norm_gain.reshape(1, -1)], flops=2 * BLOCK * D * D,
    )
    bank = x_in[:, D + 16 :].reshape(XS * ZS, K, NCH, D).transpose(1, 0, 2, 3).reshape(K * NSEQ * NCH, D)
    context = exchange(context, "ch")
    bank_mine, bank_theirs = spread_down(bank)
    context, predicted = call(
        predict_kernel, [shape((LEN, CIN), BF16), shape((K, LEN, CIN), BF16)], [context, w_pred],
        flops=K * 2 * LEN * CIN * CIN,
    )
    (loss,) = call(
        loss_kernel, [shape((K, LEN), F32)], [predicted, window, halo, masks, *bank_mine, *bank_theirs],
        away=(2,),
        flops=K * 2 * LEN * CIN * 256,
        scratch=[pltpu.VMEM((LEN + FAR, CIN), BF16), pltpu.VMEM(halo.shape, BF16), pltpu.SemaphoreType.DMA],
    )
    return context, loss


def solution(mesh):
    placed = (
        P("seq", "ch"),
        P("ch", None),
        P(None, BOTH),
        P(),
        P(),
        P(BOTH),
        P(None, BOTH),
    )
    return jax.shard_map(
        lambda *a: tuple(step(*a)),
        mesh=mesh,
        in_specs=placed,
        out_specs=(P(BOTH, None), P(None, BOTH)),
        check_vma=False,
    )
```
